32 devices in a mesh: occ: 4 (over y, x), sec: 8 (over z, core).
Axes of the slice: x: 2, y: 2, z: 4, core: 2. Of those that a mesh axis runs over, the one named last changes fastest.
Arguments:
- amplitudes: float32 [192, 512, 512], P('occ', None, 'sec'), may hold values from -5 to 5
- live_pairs: int32 [4], replicated, may hold values from 12 to 48, as said below
- ladder_ints: float32 [512, 512, 1024], P('occ', 'sec'), may hold values from -0.015625 to 0.015625
- cycle_ints: float32 [48, 512, 6144], P(None, 'sec', 'occ'), may hold values from -0.0390625 to 0.0390625
- pair_ints: float32 [192, 1024], P('occ', 'sec'), may hold values from -6 to 6
- occ_energy: float32 [48], replicated, may hold values from -2 to -0.5
- vir_energy: float32 [512], replicated, may hold values from 0.5 to 4
Outputs:
- new_amplitudes: float32 [192, 1024], P('occ', 'sec')
The draws below stay inside these ranges and needn't reach their ends.
Inputs may be any that keep to these rules, and one draw needn't show every extreme that they name: live_pairs[o] live pairs are the first ones of owner o's 48 pairs; some owner has all of its pairs live.
All inputs are finite; a program needn't handle non-finite values.
Results may differ from the reference program's by a relative error of at most 0.00005.
Values sent between devices are 32-bit elements; how exact they have to be, the bound alone decides.
No kernel may reach another device: no remote copies, remote signals or barrier semaphores. Data moves between devices by JAX's collectives and lax.ppermute only.
A program may use at most 128 MiB of HBM per device.

```python
import jax
import jax.numpy as jnp
from jax import lax

OCCUPIED = 48
VIRTUAL = 512
A_WINDOW = 8
B_WINDOW = 128
OWNERS = 4
I_WINDOW = 4
PAIR_OWNER = 48
PAIRS = 192
AB_WINDOW = 1024


def draw_live_pairs(key, part):
    first_key, second_key = jax.random.split(jax.random.fold_in(key, 17))
    counts_drawn = jax.random.randint(first_key, (OWNERS,), max(1, PAIR_OWNER // 4), PAIR_OWNER + 1, dtype=jnp.int32)
    chosen = jax.random.randint(second_key, (), 0, OWNERS, dtype=jnp.int32)
    positions = jnp.arange(OWNERS, dtype=jnp.int32)
    return jnp.where(positions == chosen, PAIR_OWNER, counts_drawn).astype(jnp.int32)


def strengthened(drawn, rng, source, target, parts, factor):
    owner, partner = [(jnp.arange(drawn.shape[position]) // (drawn.shape[position] // parts)).reshape([-1 if axis == position else 1 for axis in range(drawn.ndim)]) for position in (source, target)]
    chosen = jax.random.permutation(rng, parts)[partner]
    strong = (owner == chosen) | (owner == (partner + parts // 2) % parts)
    return jnp.where(strong, factor * drawn, drawn)


def block_scale(own_key, dims, pieces, least, top_value):
    def one(dim, shards_of):
        steps = jax.random.uniform(jax.random.fold_in(jax.random.fold_in(own_key, 6), dim), (shards_of,), jnp.float32, least / len(pieces), top_value / len(pieces))
        return jnp.repeat(jnp.exp(steps), dims[dim] // shards_of).reshape((-1,) + (1,) * (len(dims) - dim - 1))

    level = one(*pieces[0])
    for cut in pieces[1:]:
        level = level * one(*cut)
    return level


def gaussian(own_key, extent, width, reach, cuts=(), held_as=jnp.bfloat16):
    array = width * jax.random.normal(own_key, extent, jnp.float32)
    if cuts:
        array = array * block_scale(own_key, extent, cuts, -0.22, 0.18)
    return jnp.clip(array, -reach, reach).astype(held_as)


def noise_with(stream_key, extent, deviation, most, cuts, heavy, kind=jnp.bfloat16):
    values = deviation * jax.random.normal(stream_key, extent, jnp.float32)
    if cuts:
        values = values * block_scale(stream_key, extent, cuts, -0.22, 0.18)
    return jnp.clip(strengthened(values, jax.random.fold_in(stream_key, 3), *heavy), -most, most).astype(kind)


def setup_inputs(seed: int = 0) -> dict:
    key_list = jax.random.split(jax.random.key(seed), 8)
    amplitudes = gaussian(key_list[0], (PAIRS, VIRTUAL, VIRTUAL), 1.0, 5.0, ((0, 4), (2, 8)), jnp.float32)
    live_pairs = draw_live_pairs(jax.random.fold_in(key_list[7], 71), 0)
    ladder_ints = noise_with(key_list[2], (VIRTUAL, VIRTUAL, AB_WINDOW), (VIRTUAL * VIRTUAL) ** -0.5, 0.015625, ((0, 4), (1, 8)), (1, 2, 8, 2.0), jnp.float32)
    cycle_ints = gaussian(key_list[3], (OCCUPIED, VIRTUAL, OCCUPIED * B_WINDOW), (OCCUPIED * VIRTUAL) ** -0.5, 0.0390625, ((1, 8), (2, 4)), jnp.float32)
    pair_ints = gaussian(key_list[4], (PAIRS, AB_WINDOW), 1.0, 6.0, ((0, 4), (1, 8)), jnp.float32)
    occ_energy = jnp.clip(jax.random.uniform(key_list[5], (OCCUPIED,), jnp.float32, -2.0, -0.5), -2.0, -0.5)
    vir_energy = jnp.clip(jax.random.uniform(key_list[6], (VIRTUAL,), jnp.float32, 0.5, 4.0), 0.5, 4.0)
    return {"amplitudes": amplitudes, "live_pairs": live_pairs, "ladder_ints": ladder_ints, "cycle_ints": cycle_ints, "pair_ints": pair_ints, "occ_energy": occ_energy, "vir_energy": vir_energy}


highest = lax.Precision.HIGHEST


def reference(amplitudes, live_pairs, ladder_ints, cycle_ints, pair_ints, occ_energy, vir_energy):
    pair_index = jnp.arange(PAIRS, dtype=jnp.int32)
    owner_of = (pair_index // PAIR_OWNER).astype(jnp.int32)
    live_mask = ((pair_index % PAIR_OWNER) < live_pairs[owner_of]).astype(jnp.float32)
    masked = amplitudes * live_mask[:, None, None]
    ladder = jnp.dot(masked.reshape(PAIRS, VIRTUAL * VIRTUAL), ladder_ints.reshape(VIRTUAL * VIRTUAL, AB_WINDOW), precision=highest, preferred_element_type=jnp.float32)
    cycle_rows = masked.reshape(I_WINDOW, OCCUPIED, VIRTUAL, VIRTUAL)[:, :, :A_WINDOW, :]
    cycle_term = jnp.einsum("ikac,kcn->ian", cycle_rows, cycle_ints, precision=highest)
    cycle_term = cycle_term.reshape(I_WINDOW, A_WINDOW, OCCUPIED, B_WINDOW).transpose(0, 2, 1, 3).reshape(PAIRS, AB_WINDOW)
    residual = pair_ints + 0.5 * ladder + cycle_term
    occ_pairs = (occ_energy[:I_WINDOW, None] + occ_energy[None, :]).reshape(PAIRS, 1)
    vir_pairs = (vir_energy[:A_WINDOW, None] + vir_energy[None, :B_WINDOW]).reshape(1, AB_WINDOW)
    return residual / (occ_pairs - vir_pairs) * live_mask[:, None]
```

```python
import functools

import jax
import jax.numpy as jnp
from jax import lax
from jax.experimental import pallas as pl
from jax.experimental.pallas import tpu as pltpu
from jax.sharding import PartitionSpec as P


OCCUPIED = 48
VIRTUAL = 512
A_WINDOW = 8
B_WINDOW = 128
I_OWNER = 1
LANES = 128
D_STEP = 8
CHUNK_UNITS = 8
CHUNKS = (0, 3, 6, 7)
CYCLE_PAD = 16


f32 = jnp.float32
bf16 = jnp.bfloat16
highest = lax.Precision.HIGHEST
VMEM_LIMIT = 48 * 1024 * 1024
SMALL_LIMIT = 16 * 1024 * 1024


def split(x):
    hi = x.astype(bf16)
    return hi, (x - hi.astype(f32)).astype(bf16)


def dot(a, b):
    return jnp.dot(a, b, preferred_element_type=f32)


def dot_split(a, w):
    rows = a.shape[0]
    a_hi, a_lo = split(a)
    w_hi, w_lo = split(w)
    both = dot(jnp.concatenate([a_hi, a_lo], axis=0), w_hi)
    return both[:rows] + both[rows:] + dot(a_hi, w_lo)


def sds(*shape):
    return jax.ShapeDtypeStruct(shape, f32)


def small(kernel, out_shape, operands, scratch=()):
    vmem = pl.BlockSpec(memory_space=pltpu.VMEM)
    outs = out_shape if isinstance(out_shape, list) else [out_shape]
    moved = 4 * sum(x.size for x in [*operands, *outs])
    return pl.pallas_call(
        kernel,
        out_shape=out_shape,
        in_specs=[vmem] * len(operands),
        out_specs=[vmem] * len(outs) if isinstance(out_shape, list) else vmem,
        scratch_shapes=list(scratch),
        compiler_params=pltpu.CompilerParams(vmem_limit_bytes=SMALL_LIMIT),
        cost_estimate=pl.CostEstimate(flops=0, bytes_accessed=moved, transcendentals=0),
    )(*operands)


def after(value, earlier):
    return lax.optimization_barrier((value, earlier))[0]


def block_of(index):
    return pl.ds(pl.multiple_of(index * LANES, LANES), LANES)


def slice_kernel(d0, a_ref, *refs):
    outs, sem = refs[:-1], refs[-1]
    owner = lax.axis_index("occ")
    copies = [
        pltpu.make_async_copy(a_ref.at[:, pl.ds(d0, out.shape[1]), block_of(owner ^ k)], out, sem.at[k - 1])
        for k, out in enumerate(outs, start=1)
    ]
    for copy in copies:
        copy.start()
    for copy in copies:
        copy.wait()


def slice_chunk(turn, flipped, owners, d0, dn):
    rows = flipped.shape[0]
    n = owners - 1
    return pl.pallas_call(
        lambda _, *refs: slice_kernel(d0, *refs),
        out_shape=[sds(rows, dn, LANES)] * n,
        in_specs=[pl.BlockSpec(memory_space=pl.ANY)] * 2,
        out_specs=[pl.BlockSpec(memory_space=pltpu.VMEM)] * n,
        scratch_shapes=[pltpu.SemaphoreType.DMA((n,))],
        compiler_params=pltpu.CompilerParams(vmem_limit_bytes=VMEM_LIMIT),
        cost_estimate=pl.CostEstimate(flops=0, bytes_accessed=8 * n * rows * dn * LANES, transcendentals=0),
        name="slices",
    )(turn, flipped)


def window_kernel(window, counts, a_ref, out_ref):
    rows, depth, _ = a_ref.shape
    flat = a_ref[...].reshape(rows * depth, LANES)
    pair = lax.broadcasted_iota(jnp.int32, (window, rows * depth), 1) // depth
    out_ref[...] = jnp.where(pair < counts[lax.axis_index("occ")], flat.T[:window], 0.0)


def cycle_window(counts, flipped, window):
    rows, depth, _ = flipped.shape
    return pl.pallas_call(
        functools.partial(window_kernel, window),
        out_shape=sds(window, rows * depth),
        grid_spec=pltpu.PrefetchScalarGridSpec(
            num_scalar_prefetch=1,
            grid=(1,),
            in_specs=[pl.BlockSpec((rows, depth, LANES), lambda i, counts: (0, 0, 0))],
            out_specs=pl.BlockSpec((window, rows * depth), lambda i, counts: (0, 0)),
        ),
        compiler_params=pltpu.CompilerParams(vmem_limit_bytes=VMEM_LIMIT),
        cost_estimate=pl.CostEstimate(flops=0, bytes_accessed=4 * rows * depth * LANES, transcendentals=0),
        name="cycle_window",
    )(counts, flipped)


def ladder_kernel(n, first, last, steps, ids, *refs):
    a_refs, w_ref, rest = refs[:n], refs[n], refs[n + 1 :]
    acc_ref = rest[-1]
    step = pl.program_id(0)

    @pl.when(step == 0)
    def _():
        acc_ref[...] = jnp.zeros_like(acc_ref) if first else rest[0][...]

    for d in range(0, D_STEP, 2):
        a = jnp.concatenate(
            [jnp.concatenate([r[:, d, :], r[:, d + 1, :]], axis=1) for r in a_refs], axis=0
        )
        w = jnp.concatenate([w_ref[:, d, :], w_ref[:, d + 1, :]], axis=0)
        acc_ref[...] += dot_split(a, w)

    if last:

        @pl.when(step == steps - 1)
        def _():
            pair_halves(acc_ref, rest[-3], rest[-2])


def pair_halves(src_ref, send_ref, keep_ref):
    core = lax.rem(lax.axis_index("sec"), 2)
    for z in range(send_ref.shape[1] // LANES):
        cols = slice(z * LANES, (z + 1) * LANES)
        send_ref[:, cols] = src_ref[:, block_of(2 * z + 1 - core)]
        keep_ref[:, cols] = src_ref[:, block_of(2 * z + core)]


def ladder_product(ids, flipped, arrived, ladder_ints, acc, d0, last):
    n = len(arrived) + 1
    rows, dn, _ = arrived[0].shape
    cols = ladder_ints.shape[2]
    first = acc is None
    steps = dn // D_STEP
    total = pl.BlockSpec((n * rows, cols), lambda i, ids: (0, 0))
    half = pl.BlockSpec((n * rows, cols // 2), lambda i, ids: (0, 0))
    return pl.pallas_call(
        functools.partial(ladder_kernel, n, first, last, steps),
        out_shape=[sds(n * rows, cols // 2)] * 2 if last else sds(n * rows, cols),
        grid_spec=pltpu.PrefetchScalarGridSpec(
            num_scalar_prefetch=1,
            grid=(steps,),
            in_specs=[pl.BlockSpec((rows, D_STEP, LANES), lambda i, ids: (0, d0 // D_STEP + i, ids[0]))]
            + [pl.BlockSpec((rows, D_STEP, LANES), lambda i, ids: (0, i, 0))] * (n - 1)
            + [pl.BlockSpec((LANES, D_STEP, cols), lambda i, ids: (0, d0 // D_STEP + i, 0))]
            + ([] if first else [total]),
            out_specs=[half] * 2 if last else total,
            scratch_shapes=[pltpu.VMEM((n * rows, cols), f32)] if last else [],
        ),
        compiler_params=pltpu.CompilerParams(vmem_limit_bytes=VMEM_LIMIT),
        cost_estimate=pl.CostEstimate(
            flops=6 * n * rows * dn * LANES * cols,
            bytes_accessed=4 * dn * LANES * cols,
            transcendentals=0,
        ),
        name="ladder_product",
    )(ids, flipped, *arrived, ladder_ints, *([] if first else [acc]))


def cycle_kernel(owners, steps, *refs):
    a_refs, u_ref, (send_ref, keep_ref, acc_ref, flat_ref) = refs[:owners], refs[owners], refs[owners + 1 :]
    step = pl.program_id(0)

    @pl.when(step == 0)
    def _():
        acc_ref[...] = jnp.zeros_like(acc_ref)
        flat_ref[...] = jnp.zeros_like(flat_ref)

    u = u_ref[...]
    a = jnp.concatenate([r[...] for r in a_refs], axis=0)
    acc_ref[...] += dot_split(a, u.reshape(u.shape[0] * u.shape[1], u.shape[2]))

    @pl.when(step == steps - 1)
    def _():
        window = acc_ref.shape[0] // owners
        for k in range(owners):
            for j in range(acc_ref.shape[1] // LANES):
                for a in range(window):
                    flat_ref[k * CYCLE_PAD + j : k * CYCLE_PAD + j + 1, a * LANES : (a + 1) * LANES] = acc_ref[
                        k * window + a : k * window + a + 1, j * LANES : (j + 1) * LANES
                    ]
        pair_halves(flat_ref, send_ref, keep_ref)


def cycle_product(windows, cycle_ints):
    owners = len(windows)
    window, depth = windows[0].shape
    ks, cs, cols = cycle_ints.shape
    kb = 8
    steps = ks // kb
    half = (owners * CYCLE_PAD, window * LANES // 2)
    return pl.pallas_call(
        functools.partial(cycle_kernel, owners, steps),
        out_shape=[sds(*half)] * 2,
        grid=(steps,),
        in_specs=[pl.BlockSpec((window, kb * cs), lambda i: (0, i))] * owners
        + [pl.BlockSpec((kb, cs, cols), lambda i: (i, 0, 0))],
        out_specs=[pl.BlockSpec(half, lambda i: (0, 0))] * 2,
        scratch_shapes=[
            pltpu.VMEM((owners * window, cols), f32),
            pltpu.VMEM((owners * CYCLE_PAD, window * LANES), f32),
        ],
        compiler_params=pltpu.CompilerParams(vmem_limit_bytes=VMEM_LIMIT),
        cost_estimate=pl.CostEstimate(
            flops=6 * owners * window * depth * cols, bytes_accessed=4 * depth * cols, transcendentals=0
        ),
        name="cycle_product",
    )(*windows, cycle_ints)


def add_blocks_kernel(keep_ref, recv_ref, *outs):
    rows = outs[0].shape[0]
    for k, out in enumerate(outs):
        part = slice(k * rows, (k + 1) * rows)
        out[...] = keep_ref[part] + recv_ref[part]


def add_blocks(keep, recv, n):
    rows, cols = keep.shape
    return small(add_blocks_kernel, [sds(rows // n, cols)] * n, [keep, recv])


def line_kernel(owners, owner_cols, *refs):
    blocks, terms, outs, all_ref = refs[:owners], refs[owners : 2 * owners], refs[2 * owners : -1], refs[-1]
    owner = lax.axis_index("occ")
    total = terms[0][...]
    for t in terms[1:]:
        total = total + t[...]
    all_ref[...] = 0.5 * total
    for k, src in enumerate(blocks):
        offset = (owner ^ k) * owner_cols
        for j in range(owner_cols):
            all_ref[pl.ds(offset + j, 1), :] += src[j : j + 1, :]
    z = lax.axis_index("sec") // 2
    for q, out in enumerate(outs):
        out[...] = all_ref[:, block_of(z ^ q)]


def final_kernel(*refs):
    *terms, pair_ref, den_ref, live_ref, out_ref = refs
    total = pair_ref[...]
    for t in terms:
        total = total + t[...]
    out_ref[...] = total / den_ref[...] * live_ref[...]


def streamed_parts(amplitudes, live_pairs, ladder_ints, cycle_ints, pair_ints, occ_energy, vir_energy):
    owners = lax.axis_size("occ")
    sections = lax.axis_size("sec")
    owner_index = lax.axis_index("occ")
    section = lax.axis_index("sec")
    owner_rows = I_OWNER * OCCUPIED
    owner_cols = OCCUPIED // owners
    col_share = A_WINDOW * B_WINDOW // sections
    d_share = amplitudes.shape[2]
    ids = owner_index.reshape(1).astype(jnp.int32)
    flipped = amplitudes.transpose(0, 2, 1)
    live_count = lax.dynamic_slice_in_dim(live_pairs, owner_index, 1)[0]

    def exchange(values):
        return [
            lax.ppermute(value, "occ", [(o, o ^ k) for o in range(owners)])
            for k, value in enumerate(values, start=1)
        ]

    def swap_pair(value):
        return lax.ppermute(value, "sec", [(s, s ^ 1) for s in range(sections)])

    starts = [d_share * c // CHUNK_UNITS for c in CHUNKS]
    chunks = list(zip(starts, [*starts[1:], d_share]))
    window = cycle_window(live_pairs, flipped, A_WINDOW)
    windows = [window] + exchange([window] * (owners - 1))
    arrived = []
    turn = window
    for d0, d1 in chunks:
        pieces = slice_chunk(after(ids, turn), flipped, owners, d0, d1 - d0)
        arrived.append(exchange(pieces))
        turn = pieces[0]

    send, keep = cycle_product(windows, cycle_ints)
    recv = swap_pair(send)
    own, *sends = add_blocks(keep, recv, owners)
    blocks = [own, *exchange(sends)]

    acc = None
    turn = own
    for (d0, d1), values in zip(chunks, arrived):
        acc = ladder_product(after(ids, turn), flipped, values, ladder_ints, acc, d0, d1 == d_share)
        turn = ids
    send, keep = acc
    own, *sends = add_blocks(keep, swap_pair(send), owners)
    terms = [*blocks, own, *exchange(sends)]
    lines = sections // 2
    pieces = small(
        functools.partial(line_kernel, owners, owner_cols),
        [sds(owner_rows, LANES)] * lines,
        terms,
        [pltpu.VMEM((owner_rows, lines * LANES), f32)],
    )
    recvs = [lax.ppermute(pieces[q], "sec", [(s, s ^ (2 * q)) for s in range(sections)]) for q in range(1, lines)]

    occ_rows = lax.dynamic_slice_in_dim(occ_energy, owner_index * I_OWNER, I_OWNER)
    pair_energy = (occ_rows[:, None] + occ_energy[None, :]).reshape(owner_rows, 1)
    vir_pairs = (vir_energy[:A_WINDOW, None] + vir_energy[None, :B_WINDOW]).reshape(A_WINDOW * B_WINDOW)
    vir_cols = lax.dynamic_slice_in_dim(vir_pairs, section * col_share, col_share)
    denominator = pair_energy - vir_cols[None, :]
    live_out = (lax.broadcasted_iota(jnp.int32, (owner_rows, col_share), 0) < live_count).astype(f32)
    operands = [pieces[0], *recvs, pair_ints, denominator, live_out]
    return small(final_kernel, sds(owner_rows, col_share), operands)


def gathered(amplitudes, live_pairs, ladder_ints, cycle_ints, pair_ints, occ_energy, vir_energy):
    owners = lax.axis_size("occ")
    sections = lax.axis_size("sec")
    owner_index = lax.axis_index("occ")
    section = lax.axis_index("sec")
    owner_rows = I_OWNER * OCCUPIED
    window_rows = I_OWNER * owners
    owner_cols = OCCUPIED // owners
    col_share = A_WINDOW * B_WINDOW // sections
    d_share = amplitudes.shape[2]
    live_count = lax.dynamic_slice_in_dim(live_pairs, owner_index, 1)[0]
    local_rows = lax.broadcasted_iota(jnp.int32, (owner_rows, 1, 1), 0)
    live_rows = (local_rows < live_count).astype(jnp.float32)
    masked = amplitudes * live_rows
    flat_tiles = masked.reshape(owner_rows, owners, VIRTUAL // owners * d_share)
    regrouped = lax.all_to_all(flat_tiles, "occ", split_axis=1, concat_axis=0, tiled=True)
    pair_total = regrouped.shape[0]
    ladder_part = 0.5 * jnp.dot(
        regrouped.reshape(pair_total, -1),
        ladder_ints.reshape(-1, A_WINDOW * B_WINDOW),
        precision=highest,
        preferred_element_type=jnp.float32,
    )
    cycle_local = masked[:, :A_WINDOW, :].reshape(owner_rows, A_WINDOW * d_share)
    cycle_flat = lax.all_gather(cycle_local, "occ", axis=0, tiled=True)
    cycle_rows = cycle_flat.reshape(window_rows, OCCUPIED, A_WINDOW, d_share)
    cycle_part = jnp.einsum(
        "ikac,kcn->ian",
        cycle_rows,
        cycle_ints,
        precision=highest,
        preferred_element_type=jnp.float32,
    )
    cycle_part = (
        cycle_part.reshape(window_rows, A_WINDOW, owner_cols, B_WINDOW)
        .transpose(0, 2, 1, 3)
        .reshape(window_rows, owner_cols, A_WINDOW * B_WINDOW)
    )
    ladder_grid = ladder_part.reshape(window_rows, OCCUPIED, A_WINDOW * B_WINDOW)
    offset = owner_index * owner_cols
    current_part = lax.dynamic_slice_in_dim(ladder_grid, offset, owner_cols, 1)
    ladder_grid = lax.dynamic_update_slice_in_dim(ladder_grid, current_part + cycle_part, offset, 1)
    combined = ladder_grid.reshape(pair_total, A_WINDOW * B_WINDOW)
    first_sum = lax.psum_scatter(combined, "sec", scatter_dimension=1, tiled=True)
    summed = lax.psum_scatter(first_sum, "occ", scatter_dimension=0, tiled=True)
    residual = summed + pair_ints
    occ_rows = lax.dynamic_slice_in_dim(occ_energy, owner_index * I_OWNER, I_OWNER)
    pair_energy = (occ_rows[:, None] + occ_energy[None, :]).reshape(owner_rows, 1)
    vir_pairs = (vir_energy[:A_WINDOW, None] + vir_energy[None, :B_WINDOW]).reshape(
        A_WINDOW * B_WINDOW
    )
    vir_cols = lax.dynamic_slice_in_dim(vir_pairs, section * col_share, col_share)
    denominator = pair_energy - vir_cols[None, :]
    live_out = (lax.broadcasted_iota(jnp.int32, (owner_rows, 1), 0) < live_count).astype(
        jnp.float32
    )
    return residual / denominator * live_out


def power_of_two(n):
    return n & (n - 1) == 0


def streams(owners, sections):
    return (
        1 < owners
        and power_of_two(owners)
        and 2 < sections
        and power_of_two(sections)
        and VIRTUAL == owners * LANES
        and A_WINDOW * B_WINDOW == sections * LANES
        and B_WINDOW == LANES
        and OCCUPIED // owners <= CYCLE_PAD
        and sections // 2 == owners
        and VIRTUAL // sections % (D_STEP * CHUNK_UNITS) == 0
    )


def solution(mesh):
    in_specs = (
        P("occ", None, "sec"),
        P(),
        P("occ", "sec", None),
        P(None, "sec", "occ"),
        P("occ", "sec"),
        P(),
        P(),
    )
    out_specs = P("occ", "sec")
    if not streams(mesh.shape["occ"], mesh.shape["sec"]):
        return jax.shard_map(gathered, mesh=mesh, in_specs=in_specs, out_specs=out_specs, check_vma=False)
    return jax.shard_map(streamed_parts, mesh=mesh, in_specs=in_specs, out_specs=out_specs, check_vma=False)
```

```python
import functools

import jax
import jax.numpy as jnp
from jax import lax
from jax.experimental import pallas as pl
from jax.experimental.pallas import tpu as pltpu
from jax.sharding import PartitionSpec as P


OCCUPIED = 48
VIRTUAL = 512
A_WINDOW = 8
B_WINDOW = 128
I_OWNER = 1
LANES = 128
D_STEP = 8
CHUNK_UNITS = 8
CHUNKS = (0, 1, 5, 7)
CYCLE_PAD = 16


f32 = jnp.float32
bf16 = jnp.bfloat16
highest = lax.Precision.HIGHEST
VMEM_LIMIT = 48 * 1024 * 1024
SMALL_LIMIT = 24 * 1024 * 1024


def split(x):
    hi = x.astype(bf16)
    return hi, (x - hi.astype(f32)).astype(bf16)


def dot(a, b):
    return jnp.dot(a, b, preferred_element_type=f32)


def dot_split(a, w_hi, w_lo):
    rows = a.shape[0]
    a_hi, a_lo = split(a)
    both = dot(jnp.concatenate([a_hi, a_lo], axis=0), w_hi)
    return both[:rows] + both[rows:] + dot(a_hi, w_lo)


def sds(*shape):
    return jax.ShapeDtypeStruct(shape, f32)


def small(kernel, out_shape, operands, scratch=()):
    vmem = pl.BlockSpec(memory_space=pltpu.VMEM)
    outs = out_shape if isinstance(out_shape, list) else [out_shape]
    moved = 4 * sum(x.size for x in [*operands, *outs])
    return pl.pallas_call(
        kernel,
        out_shape=out_shape,
        in_specs=[vmem] * len(operands),
        out_specs=[vmem] * len(outs) if isinstance(out_shape, list) else vmem,
        scratch_shapes=list(scratch),
        compiler_params=pltpu.CompilerParams(vmem_limit_bytes=SMALL_LIMIT),
        cost_estimate=pl.CostEstimate(flops=0, bytes_accessed=moved, transcendentals=0),
    )(*operands)


def after(value, earlier):
    return lax.optimization_barrier((value, earlier))[0]


def block_of(index):
    return pl.ds(pl.multiple_of(index * LANES, LANES), LANES)


def slice_kernel(d0, first, turn_ref, a_ref, *refs):
    outs, sem = refs[:-1], refs[-1]
    owner = lax.axis_index("occ")
    copies = [
        pltpu.make_async_copy(a_ref.at[:, pl.ds(d0, out.shape[1]), block_of(owner ^ k)], out, sem.at[k - first])
        for k, out in enumerate(outs, start=first)
    ]
    for copy in copies:
        copy.start()
    for copy in copies:
        copy.wait()


def slice_chunk(turn, flipped, owners, d0, dn, first=1):
    rows = flipped.shape[0]
    n = owners - first
    return pl.pallas_call(
        functools.partial(slice_kernel, d0, first),
        out_shape=[sds(rows, dn, LANES)] * n,
        in_specs=[pl.BlockSpec(memory_space=pl.ANY)] * 2,
        out_specs=[pl.BlockSpec(memory_space=pltpu.VMEM)] * n,
        scratch_shapes=[pltpu.SemaphoreType.DMA((n,))],
        compiler_params=pltpu.CompilerParams(vmem_limit_bytes=VMEM_LIMIT),
        cost_estimate=pl.CostEstimate(flops=0, bytes_accessed=8 * n * rows * dn * LANES, transcendentals=0),
        name="slices",
    )(turn, flipped)


def window_kernel(turn_ref, counts, a_ref, out_ref, tile_ref, sem):
    parts, rows, depth, _ = tile_ref.shape
    copies = [
        pltpu.make_async_copy(a_ref.at[pl.ds(p * rows, rows), :, pl.ds(0, LANES)], tile_ref.at[p], sem.at[p])
        for p in range(parts)
    ]
    for copy in copies:
        copy.start()
    live = counts[lax.axis_index("occ")]
    window = out_ref.shape[1]
    per_tile = LANES // depth
    pair = lax.broadcasted_iota(jnp.int32, (window, LANES), 1) // depth
    for p, copy in enumerate(copies):
        copy.wait()
        for t in range(rows // per_tile):
            flat = tile_ref[p, pl.ds(t * per_tile, per_tile)].reshape(LANES, LANES)
            tile = p * (rows // per_tile) + t
            out_ref[tile] = jnp.where(pair + tile * per_tile < live, flat.T[:window], 0.0)


def cycle_window(turn, counts, flipped, window):
    rows, depth, _ = flipped.shape
    hbm = pl.BlockSpec(memory_space=pl.ANY)
    return pl.pallas_call(
        window_kernel,
        out_shape=sds(rows * depth // LANES, window, LANES),
        in_specs=[hbm, pl.BlockSpec(memory_space=pltpu.SMEM), hbm],
        out_specs=pl.BlockSpec(memory_space=pltpu.VMEM),
        scratch_shapes=[pltpu.VMEM((4, rows // 4, depth, LANES), f32), pltpu.SemaphoreType.DMA((4,))],
        compiler_params=pltpu.CompilerParams(vmem_limit_bytes=VMEM_LIMIT),
        cost_estimate=pl.CostEstimate(flops=0, bytes_accessed=4 * rows * depth * LANES, transcendentals=0),
        name="cycle_window",
    )(turn, counts, flipped)


def two_steps(refs, d):
    return jnp.concatenate([jnp.concatenate([r[:, d, :], r[:, d + 1, :]], axis=1) for r in refs], axis=0)


def ladder_kernel(n, first, ids, *refs):
    a_refs, w_ref, rest = refs[:n], refs[n], refs[n + 1 :]
    acc_ref = rest[-1]

    @pl.when(pl.program_id(0) == 0)
    def _():
        acc_ref[...] = jnp.zeros_like(acc_ref) if first else rest[0][...]

    for d in range(0, D_STEP, 2):
        w = jnp.concatenate([w_ref[:, d, :], w_ref[:, d + 1, :]], axis=0)
        acc_ref[...] += dot_split(two_steps(a_refs, d), *split(w))


def pair_halves(src_ref, send_ref, keep_ref):
    core = lax.rem(lax.axis_index("sec"), 2)
    for z in range(send_ref.shape[1] // LANES):
        cols = slice(z * LANES, (z + 1) * LANES)
        send_ref[:, cols] = src_ref[:, block_of(2 * z + 1 - core)]
        keep_ref[:, cols] = src_ref[:, block_of(2 * z + core)]


def ladder_product(ids, flipped, arrived, ladder_ints, acc, d0, dn):
    n = len(arrived) + 1
    rows = flipped.shape[0]
    cols = ladder_ints.shape[2]
    first = acc is None
    total = pl.BlockSpec((n * rows, cols), lambda i, ids: (0, 0))
    return pl.pallas_call(
        functools.partial(ladder_kernel, n, first),
        out_shape=sds(n * rows, cols),
        grid_spec=pltpu.PrefetchScalarGridSpec(
            num_scalar_prefetch=1,
            grid=(dn // D_STEP,),
            in_specs=[pl.BlockSpec((rows, D_STEP, LANES), lambda i, ids: (0, d0 // D_STEP + i, ids[0]))]
            + [pl.BlockSpec((rows, D_STEP, LANES), lambda i, ids: (0, i, 0))] * (n - 1)
            + [pl.BlockSpec((LANES, D_STEP, cols), lambda i, ids: (0, d0 // D_STEP + i, 0))]
            + ([] if first else [total]),
            out_specs=total,
        ),
        compiler_params=pltpu.CompilerParams(vmem_limit_bytes=VMEM_LIMIT),
        cost_estimate=pl.CostEstimate(
            flops=6 * n * rows * dn * LANES * cols,
            bytes_accessed=4 * dn * LANES * cols,
            transcendentals=0,
        ),
        name="ladder_product",
    )(ids, flipped, *arrived, ladder_ints, *([] if first else [acc]))


def fetch_kernel(d0, turn_ref, w_ref, hi_ref, lo_ref, raw_ref, sem):
    copies = [
        pltpu.make_async_copy(w_ref.at[:, d0 + d, :], raw_ref.at[d], sem.at[d]) for d in range(raw_ref.shape[0])
    ]
    for copy in copies:
        copy.start()
    for d, copy in enumerate(copies):
        copy.wait()
        hi_ref[d], lo_ref[d] = split(raw_ref[d])


def fetch_integrals(turn, ladder_ints, d0):
    depth, _, cols = ladder_ints.shape
    vmem = pl.BlockSpec(memory_space=pltpu.VMEM)
    return pl.pallas_call(
        functools.partial(fetch_kernel, d0),
        out_shape=[jax.ShapeDtypeStruct((D_STEP, depth, cols), bf16)] * 2,
        in_specs=[pl.BlockSpec(memory_space=pl.ANY)] * 2,
        out_specs=[vmem] * 2,
        scratch_shapes=[pltpu.VMEM((D_STEP, depth, cols), f32), pltpu.SemaphoreType.DMA((D_STEP,))],
        compiler_params=pltpu.CompilerParams(vmem_limit_bytes=SMALL_LIMIT),
        cost_estimate=pl.CostEstimate(flops=0, bytes_accessed=8 * D_STEP * depth * cols, transcendentals=0),
        name="fetch_integrals",
    )(turn, ladder_ints)


def closing_kernel(n, *refs):
    a_refs, (hi_ref, lo_ref, acc_in, send_ref, keep_ref, acc_ref) = refs[:n], refs[n:]
    acc_ref[...] = acc_in[...]
    for d in range(0, D_STEP, 2):
        w_hi = hi_ref[d : d + 2].reshape(2 * LANES, -1)
        w_lo = lo_ref[d : d + 2].reshape(2 * LANES, -1)
        acc_ref[...] += dot_split(two_steps(a_refs, d), w_hi, w_lo)
    pair_halves(acc_ref, send_ref, keep_ref)


def cycle_kernel(owners, steps, *refs):
    a_refs, u_ref, (send_ref, keep_ref, acc_ref, flat_ref) = refs[:owners], refs[owners], refs[owners + 1 :]
    step = pl.program_id(0)

    @pl.when(step == 0)
    def _():
        acc_ref[...] = jnp.zeros_like(acc_ref)
        flat_ref[...] = jnp.zeros_like(flat_ref)

    u = u_ref[...]
    tiles = a_refs[0].shape[0]
    a = jnp.concatenate([jnp.concatenate([r[t] for t in range(tiles)], axis=1) for r in a_refs], axis=0)
    acc_ref[...] += dot_split(a, *split(u.reshape(u.shape[0] * u.shape[1], u.shape[2])))

    @pl.when(step == steps - 1)
    def _():
        window = acc_ref.shape[0] // owners
        for k in range(owners):
            for j in range(acc_ref.shape[1] // LANES):
                for a in range(window):
                    flat_ref[k * CYCLE_PAD + j : k * CYCLE_PAD + j + 1, a * LANES : (a + 1) * LANES] = acc_ref[
                        k * window + a : k * window + a + 1, j * LANES : (j + 1) * LANES
                    ]
        pair_halves(flat_ref, send_ref, keep_ref)


def cycle_product(own, arrived, cycle_ints):
    owners = len(arrived) + 1
    tiles, window, _ = own.shape
    ks, cs, cols = cycle_ints.shape
    kb = 8
    steps = ks // kb
    per_step = tiles // steps
    half = (owners * CYCLE_PAD, window * LANES // 2)
    return pl.pallas_call(
        functools.partial(cycle_kernel, owners, steps),
        out_shape=[sds(*half)] * 2,
        grid=(steps,),
        in_specs=[pl.BlockSpec((per_step, window, LANES), lambda i: (i, 0, 0))] * owners
        + [pl.BlockSpec((kb, cs, cols), lambda i: (i, 0, 0))],
        out_specs=[pl.BlockSpec(half, lambda i: (0, 0))] * 2,
        scratch_shapes=[
            pltpu.VMEM((owners * window, cols), f32),
            pltpu.VMEM((owners * CYCLE_PAD, window * LANES), f32),
        ],
        compiler_params=pltpu.CompilerParams(vmem_limit_bytes=VMEM_LIMIT),
        cost_estimate=pl.CostEstimate(
            flops=6 * owners * window * ks * cs * cols, bytes_accessed=4 * ks * cs * cols, transcendentals=0
        ),
        name="cycle_product",
    )(own, *arrived, cycle_ints)


def add_blocks_kernel(keep_ref, recv_ref, *outs):
    rows = outs[0].shape[0]
    for k, out in enumerate(outs):
        part = slice(k * rows, (k + 1) * rows)
        out[...] = keep_ref[part] + recv_ref[part]


def add_blocks(keep, recv, n):
    rows, cols = keep.shape
    return small(add_blocks_kernel, [sds(rows // n, cols)] * n, [keep, recv])


def place_kernel(owner_cols, *refs):
    blocks, out_ref = refs[:-1], refs[-1]
    owner = lax.axis_index("occ")
    for k, src in enumerate(blocks):
        offset = (owner ^ k) * owner_cols
        for j in range(owner_cols):
            out_ref[pl.ds(offset + j, 1), :] = src[j : j + 1, :]


def line_kernel(*refs):
    half = len(refs) // 2 + 1
    cycle_ref, terms, outs = refs[0], refs[1:half], refs[half:]
    z = lax.axis_index("sec") // 2
    for q, out in enumerate(outs):
        cols = block_of(z ^ q)
        total = terms[0][:, cols]
        for t in terms[1:]:
            total = total + t[:, cols]
        out[...] = 0.5 * total + cycle_ref[:, cols]


def final_kernel(*refs):
    *terms, pair_ref, den_ref, live_ref, out_ref = refs
    total = pair_ref[...]
    for t in terms:
        total = total + t[...]
    out_ref[...] = total / den_ref[...] * live_ref[...]


def streamed_parts(amplitudes, live_pairs, ladder_ints, cycle_ints, pair_ints, occ_energy, vir_energy):
    owners = lax.axis_size("occ")
    sections = lax.axis_size("sec")
    owner_index = lax.axis_index("occ")
    section = lax.axis_index("sec")
    owner_rows = I_OWNER * OCCUPIED
    owner_cols = OCCUPIED // owners
    col_share = A_WINDOW * B_WINDOW // sections
    d_share = amplitudes.shape[2]
    ids = owner_index.reshape(1).astype(jnp.int32)
    flipped = amplitudes.transpose(0, 2, 1)
    live_count = lax.dynamic_slice_in_dim(live_pairs, owner_index, 1)[0]

    def exchange(values):
        moved = {}
        for k in reversed(range(1, owners)):
            moved[k] = lax.ppermute(values[k - 1], "occ", [(o, o ^ k) for o in range(owners)])
        return [moved[k] for k in range(1, owners)]

    def swap_pair(value):
        return lax.ppermute(value, "sec", [(s, s ^ 1) for s in range(sections)])

    starts = [d_share * c // CHUNK_UNITS for c in CHUNKS]
    chunks = [(d0, d1 - d0) for d0, d1 in zip(starts, [*starts[1:], d_share])]
    arrived = []
    turn = ids
    for c, (d0, dn) in enumerate(chunks):
        if c < len(chunks) - 1:
            pieces = slice_chunk(after(ids, turn), flipped, owners, d0, dn)
        else:
            closing_own, *pieces = slice_chunk(after(ids, turn), flipped, owners, d0, dn, 0)
        arrived.append(exchange(pieces))
        turn = pieces[0]
        if c == 0:
            window = cycle_window(after(ids, turn), live_pairs, flipped, A_WINDOW)
            windows = exchange([window] * (owners - 1))
            turn = window

    send, keep = cycle_product(window, windows, cycle_ints)
    recv = swap_pair(send)
    own, *sends = add_blocks(keep, recv, owners)
    blocks = [own, *exchange(sends)]
    cycle = small(functools.partial(place_kernel, owner_cols), sds(owner_rows, own.shape[1]), blocks)

    acc = None
    turn = own
    for c, ((d0, dn), values) in enumerate(zip(chunks[:-1], arrived)):
        acc = ladder_product(after(ids, turn), flipped, values, ladder_ints, acc, d0, dn)
        turn = ids
        if c == 0:
            parts = fetch_integrals(after(ids, acc), ladder_ints, chunks[-1][0])
            turn = parts[0]
    send, keep = small(
        functools.partial(closing_kernel, owners),
        [sds(acc.shape[0], acc.shape[1] // 2)] * 2,
        [closing_own, *arrived[-1], *parts, acc],
        [pltpu.VMEM(acc.shape, f32)],
    )
    own, *sends = add_blocks(keep, swap_pair(send), owners)
    terms = [cycle, own, *exchange(sends)]
    lines = sections // 2
    pieces = small(line_kernel, [sds(owner_rows, LANES)] * lines, terms)
    recvs = [
        lax.ppermute(pieces[q], "sec", [(s, s ^ (2 * q)) for s in range(sections)]) for q in reversed(range(1, lines))
    ]

    occ_rows = lax.dynamic_slice_in_dim(occ_energy, owner_index * I_OWNER, I_OWNER)
    pair_energy = (occ_rows[:, None] + occ_energy[None, :]).reshape(owner_rows, 1)
    vir_pairs = (vir_energy[:A_WINDOW, None] + vir_energy[None, :B_WINDOW]).reshape(A_WINDOW * B_WINDOW)
    vir_cols = lax.dynamic_slice_in_dim(vir_pairs, section * col_share, col_share)
    denominator = pair_energy - vir_cols[None, :]
    live_out = (lax.broadcasted_iota(jnp.int32, (owner_rows, col_share), 0) < live_count).astype(f32)
    operands = [pieces[0], *recvs, pair_ints, denominator, live_out]
    return small(final_kernel, sds(owner_rows, col_share), operands)


def gathered(amplitudes, live_pairs, ladder_ints, cycle_ints, pair_ints, occ_energy, vir_energy):
    owners = lax.axis_size("occ")
    sections = lax.axis_size("sec")
    owner_index = lax.axis_index("occ")
    section = lax.axis_index("sec")
    owner_rows = I_OWNER * OCCUPIED
    window_rows = I_OWNER * owners
    owner_cols = OCCUPIED // owners
    col_share = A_WINDOW * B_WINDOW // sections
    d_share = amplitudes.shape[2]
    live_count = lax.dynamic_slice_in_dim(live_pairs, owner_index, 1)[0]
    local_rows = lax.broadcasted_iota(jnp.int32, (owner_rows, 1, 1), 0)
    live_rows = (local_rows < live_count).astype(jnp.float32)
    masked = amplitudes * live_rows
    flat_tiles = masked.reshape(owner_rows, owners, VIRTUAL // owners * d_share)
    regrouped = lax.all_to_all(flat_tiles, "occ", split_axis=1, concat_axis=0, tiled=True)
    pair_total = regrouped.shape[0]
    ladder_part = 0.5 * jnp.dot(
        regrouped.reshape(pair_total, -1),
        ladder_ints.reshape(-1, A_WINDOW * B_WINDOW),
        precision=highest,
        preferred_element_type=jnp.float32,
    )
    cycle_local = masked[:, :A_WINDOW, :].reshape(owner_rows, A_WINDOW * d_share)
    cycle_flat = lax.all_gather(cycle_local, "occ", axis=0, tiled=True)
    cycle_rows = cycle_flat.reshape(window_rows, OCCUPIED, A_WINDOW, d_share)
    cycle_part = jnp.einsum(
        "ikac,kcn->ian",
        cycle_rows,
        cycle_ints,
        precision=highest,
        preferred_element_type=jnp.float32,
    )
    cycle_part = (
        cycle_part.reshape(window_rows, A_WINDOW, owner_cols, B_WINDOW)
        .transpose(0, 2, 1, 3)
        .reshape(window_rows, owner_cols, A_WINDOW * B_WINDOW)
    )
    ladder_grid = ladder_part.reshape(window_rows, OCCUPIED, A_WINDOW * B_WINDOW)
    offset = owner_index * owner_cols
    current_part = lax.dynamic_slice_in_dim(ladder_grid, offset, owner_cols, 1)
    ladder_grid = lax.dynamic_update_slice_in_dim(ladder_grid, current_part + cycle_part, offset, 1)
    combined = ladder_grid.reshape(pair_total, A_WINDOW * B_WINDOW)
    first_sum = lax.psum_scatter(combined, "sec", scatter_dimension=1, tiled=True)
    summed = lax.psum_scatter(first_sum, "occ", scatter_dimension=0, tiled=True)
    residual = summed + pair_ints
    occ_rows = lax.dynamic_slice_in_dim(occ_energy, owner_index * I_OWNER, I_OWNER)
    pair_energy = (occ_rows[:, None] + occ_energy[None, :]).reshape(owner_rows, 1)
    vir_pairs = (vir_energy[:A_WINDOW, None] + vir_energy[None, :B_WINDOW]).reshape(
        A_WINDOW * B_WINDOW
    )
    vir_cols = lax.dynamic_slice_in_dim(vir_pairs, section * col_share, col_share)
    denominator = pair_energy - vir_cols[None, :]
    live_out = (lax.broadcasted_iota(jnp.int32, (owner_rows, 1), 0) < live_count).astype(
        jnp.float32
    )
    return residual / denominator * live_out


def power_of_two(n):
    return n & (n - 1) == 0


def streams(owners, sections):
    return (
        1 < owners
        and power_of_two(owners)
        and 2 < sections
        and power_of_two(sections)
        and VIRTUAL == owners * LANES
        and A_WINDOW * B_WINDOW == sections * LANES
        and B_WINDOW == LANES
        and OCCUPIED // owners <= CYCLE_PAD
        and A_WINDOW == D_STEP
        and LANES % (VIRTUAL // sections) == 0
        and sections // 2 == owners
        and VIRTUAL // sections % (D_STEP * CHUNK_UNITS) == 0
    )


def solution(mesh):
    in_specs = (
        P("occ", None, "sec"),
        P(),
        P("occ", "sec", None),
        P(None, "sec", "occ"),
        P("occ", "sec"),
        P(),
        P(),
    )
    out_specs = P("occ", "sec")
    if not streams(mesh.shape["occ"], mesh.shape["sec"]):
        return jax.shard_map(gathered, mesh=mesh, in_specs=in_specs, out_specs=out_specs, check_vma=False)
    return jax.shard_map(streamed_parts, mesh=mesh, in_specs=in_specs, out_specs=out_specs, check_vma=False)
```

```python
import functools

import jax
import jax.numpy as jnp
from jax import lax
from jax.experimental import pallas as pl
from jax.experimental.pallas import tpu as pltpu
from jax.sharding import PartitionSpec as P


OCCUPIED = 48
VIRTUAL = 512
A_WINDOW = 8
B_WINDOW = 128
I_OWNER = 1
LANES = 128
D_STEP = 8
CHUNK_UNITS = 8
CHUNKS = (0, 1, 5, 7)
CYCLE_PAD = 16


f32 = jnp.float32
bf16 = jnp.bfloat16
highest = lax.Precision.HIGHEST
VMEM_LIMIT = 48 * 1024 * 1024
SMALL_LIMIT = 24 * 1024 * 1024


def split(x):
    hi = x.astype(bf16)
    return hi, (x - hi.astype(f32)).astype(bf16)


def dot(a, b):
    return jnp.dot(a, b, preferred_element_type=f32)


def dot_split(a, w_hi, w_lo):
    rows = a.shape[0]
    a_hi, a_lo = split(a)
    both = dot(jnp.concatenate([a_hi, a_lo], axis=0), w_hi)
    return both[:rows] + both[rows:] + dot(a_hi, w_lo)


def sds(*shape):
    return jax.ShapeDtypeStruct(shape, f32)


def small(kernel, out_shape, operands, scratch=()):
    vmem = pl.BlockSpec(memory_space=pltpu.VMEM)
    outs = out_shape if isinstance(out_shape, list) else [out_shape]
    moved = 4 * sum(x.size for x in [*operands, *outs])
    return pl.pallas_call(
        kernel,
        out_shape=out_shape,
        in_specs=[vmem] * len(operands),
        out_specs=[vmem] * len(outs) if isinstance(out_shape, list) else vmem,
        scratch_shapes=list(scratch),
        compiler_params=pltpu.CompilerParams(vmem_limit_bytes=SMALL_LIMIT),
        cost_estimate=pl.CostEstimate(flops=0, bytes_accessed=moved, transcendentals=0),
    )(*operands)


def after(value, earlier):
    return lax.optimization_barrier((value, earlier))[0]


def block_of(index):
    return pl.ds(pl.multiple_of(index * LANES, LANES), LANES)


def slice_kernel(d0, turn_ref, a_ref, *refs):
    outs, sem = refs[:-1], refs[-1]
    owner = lax.axis_index("occ")
    copies = [
        pltpu.make_async_copy(a_ref.at[:, pl.ds(d0, out.shape[1]), block_of(owner ^ k)], out, sem.at[k - 1])
        for k, out in enumerate(outs, start=1)
    ]
    for copy in copies:
        copy.start()
    for copy in copies:
        copy.wait()


def slice_chunk(turn, flipped, owners, d0, dn):
    rows = flipped.shape[0]
    n = owners - 1
    return pl.pallas_call(
        functools.partial(slice_kernel, d0),
        out_shape=[sds(rows, dn, LANES)] * n,
        in_specs=[pl.BlockSpec(memory_space=pl.ANY)] * 2,
        out_specs=[pl.BlockSpec(memory_space=pltpu.VMEM)] * n,
        scratch_shapes=[pltpu.SemaphoreType.DMA((n,))],
        compiler_params=pltpu.CompilerParams(vmem_limit_bytes=VMEM_LIMIT),
        cost_estimate=pl.CostEstimate(flops=0, bytes_accessed=8 * n * rows * dn * LANES, transcendentals=0),
        name="slices",
    )(turn, flipped)


def window_kernel(turn_ref, counts, a_ref, out_ref, tile_ref, sem):
    parts, rows, depth, _ = tile_ref.shape
    copies = [
        pltpu.make_async_copy(a_ref.at[pl.ds(p * rows, rows), :, pl.ds(0, LANES)], tile_ref.at[p], sem.at[p])
        for p in range(parts)
    ]
    for copy in copies:
        copy.start()
    live = counts[lax.axis_index("occ")]
    window = out_ref.shape[1]
    per_tile = LANES // depth
    pair = lax.broadcasted_iota(jnp.int32, (window, LANES), 1) // depth
    for p, copy in enumerate(copies):
        copy.wait()
        for t in range(rows // per_tile):
            flat = tile_ref[p, pl.ds(t * per_tile, per_tile)].reshape(LANES, LANES)
            tile = p * (rows // per_tile) + t
            out_ref[tile] = jnp.where(pair + tile * per_tile < live, flat.T[:window], 0.0)


def cycle_window(turn, counts, flipped, window):
    rows, depth, _ = flipped.shape
    hbm = pl.BlockSpec(memory_space=pl.ANY)
    return pl.pallas_call(
        window_kernel,
        out_shape=sds(rows * depth // LANES, window, LANES),
        in_specs=[hbm, pl.BlockSpec(memory_space=pltpu.SMEM), hbm],
        out_specs=pl.BlockSpec(memory_space=pltpu.VMEM),
        scratch_shapes=[pltpu.VMEM((4, rows // 4, depth, LANES), f32), pltpu.SemaphoreType.DMA((4,))],
        compiler_params=pltpu.CompilerParams(vmem_limit_bytes=VMEM_LIMIT),
        cost_estimate=pl.CostEstimate(flops=0, bytes_accessed=4 * rows * depth * LANES, transcendentals=0),
        name="cycle_window",
    )(turn, counts, flipped)


def side_by_side(refs):
    return jnp.concatenate([jnp.concatenate([r[:, d, :] for d in range(D_STEP)], axis=1) for r in refs], axis=0)


def gather_copies(w_ref, buf_ref, sem, block, slot):
    return [
        pltpu.make_async_copy(w_ref.at[:, block * D_STEP + d, :], buf_ref.at[slot, d], sem.at[slot, d])
        for d in range(D_STEP)
    ]


def ladder_kernel(block0, steps, own, last, n, turn, *refs):
    own_refs, refs = refs[:own], refs[own:]
    groups = [refs[g * n : (g + 1) * n] for g in range(len(steps))]
    w_ref, rest = refs[len(steps) * n], refs[len(steps) * n + 1 :]
    buf_ref, sem = rest[-2:]
    acc_in, outs = rest[: 1 if own or last else 0], rest[1 if own or last else 0 : -2]
    acc_ref = outs[-1]
    own_rows = own_refs[0].shape[0] if own else 0
    step, count = pl.program_id(0), pl.num_programs(0)
    slot = lax.rem(step, 2)

    @pl.when(step == 0)
    def _():
        for copy in gather_copies(w_ref, buf_ref, sem, block0, 0):
            copy.start()
        if last:
            acc_ref[...] = acc_in[0][...]
        else:
            acc_ref[own_rows:] = jnp.zeros((acc_ref.shape[0] - own_rows, acc_ref.shape[1]), f32)
        if own:
            acc_ref[:own_rows] = acc_in[0][...]

    @pl.when(step + 1 < count)
    def _():
        for copy in gather_copies(w_ref, buf_ref, sem, block0 + step + 1, 1 - slot):
            copy.start()

    for copy in gather_copies(w_ref, buf_ref, sem, block0 + step, slot):
        copy.wait()

    a = side_by_side(groups[-1])
    bound = sum(steps)
    for g in reversed(range(len(steps) - 1)):
        bound -= steps[g + 1]
        a = jnp.where(step < bound, side_by_side(groups[g]), a)
    if own:
        a = jnp.concatenate([side_by_side(own_refs), a], axis=0)
    w = buf_ref[slot].reshape(D_STEP * LANES, -1)
    acc_ref[...] += dot_split(a, *split(w))

    @pl.when(step == count - 1)
    def _():
        if last:
            pair_halves(acc_ref, outs[0], outs[1])
        if own:
            pair_halves(acc_ref.at[pl.ds(0, own_rows)], outs[0], outs[1])
            outs[2][...] = acc_ref[own_rows:]


def pair_halves(src_ref, send_ref, keep_ref):
    core = lax.rem(lax.axis_index("sec"), 2)
    for z in range(send_ref.shape[1] // LANES):
        cols = slice(z * LANES, (z + 1) * LANES)
        send_ref[:, cols] = src_ref[:, block_of(2 * z + 1 - core)]
        keep_ref[:, cols] = src_ref[:, block_of(2 * z + core)]


def ladder_product(turn, groups, ladder_ints, d0, own=None, acc=None, lanes=False):
    n = len(groups[0])
    rows = groups[0][0].shape[0]
    depth, _, cols = ladder_ints.shape
    with_own, last = own is not None, own is None and acc is not None
    steps = [group[0].shape[1] // D_STEP for group in groups]
    block0 = d0 // D_STEP
    if lanes:
        steps = [steps[0] - block0]
    count = sum(steps)

    def total(rows, cols):
        return sds(rows, cols), pl.BlockSpec((rows, cols), lambda i, turn: (0, 0))

    def rows_spec(g):
        before = sum(steps[:g])
        return pl.BlockSpec((rows, D_STEP, LANES), lambda i, turn: (0, jnp.clip(i - before, 0, steps[g] - 1), 0))

    own_spec = pl.BlockSpec((rows, D_STEP, LANES), lambda i, turn: (0, block0 + i, turn[0]))
    if with_own:
        outs = [total(rows, cols // 2)] * 2 + [total(n * rows, cols)]
    else:
        outs = [total(n * rows, cols // 2)] * 2 if last else [total(n * rows, cols)]
    all_rows = (n + with_own) * rows
    return pl.pallas_call(
        functools.partial(ladder_kernel, block0, steps, with_own, last, n),
        out_shape=[shape for shape, _ in outs],
        grid_spec=pltpu.PrefetchScalarGridSpec(
            num_scalar_prefetch=1,
            grid=(count,),
            in_specs=[own_spec] * with_own
            + [own_spec if lanes else rows_spec(g) for g in range(len(groups)) for _ in range(n)]
            + [pl.BlockSpec(memory_space=pl.ANY)]
            + ([] if acc is None else [total(*acc.shape)[1]]),
            out_specs=[spec for _, spec in outs],
            scratch_shapes=([pltpu.VMEM((all_rows, cols), f32)] if with_own or last else [])
            + [pltpu.VMEM((2, D_STEP, depth, cols), f32), pltpu.SemaphoreType.DMA((2, D_STEP))],
        ),
        compiler_params=pltpu.CompilerParams(vmem_limit_bytes=VMEM_LIMIT),
        cost_estimate=pl.CostEstimate(
            flops=6 * all_rows * count * D_STEP * depth * cols,
            bytes_accessed=4 * count * D_STEP * depth * cols,
            transcendentals=0,
        ),
        name="ladder_product",
    )(
        turn,
        *([own] if with_own else []),
        *[value for group in groups for value in group],
        ladder_ints,
        *([] if acc is None else [acc]),
    )


def fetch_kernel(d0, turn_ref, w_ref, *refs):
    send_refs, keep_refs, (raw_ref, sem) = refs[:2], refs[2:4], refs[4:]
    copies = [
        pltpu.make_async_copy(w_ref.at[:, d0 + d, :], raw_ref.at[d], sem.at[d]) for d in range(raw_ref.shape[0])
    ]
    for copy in copies:
        copy.start()
    core = lax.rem(lax.axis_index("sec"), 2)
    for d, copy in enumerate(copies):
        copy.wait()
        for z in range(send_refs[0].shape[2] // LANES):
            cols = slice(z * LANES, (z + 1) * LANES)
            send_refs[0][d, :, cols], send_refs[1][d, :, cols] = split(raw_ref[d, :, block_of(2 * z + 1 - core)])
            keep_refs[0][d, :, cols], keep_refs[1][d, :, cols] = split(raw_ref[d, :, block_of(2 * z + core)])


def fetch_integrals(turn, ladder_ints, d0):
    depth, _, cols = ladder_ints.shape
    vmem = pl.BlockSpec(memory_space=pltpu.VMEM)
    return pl.pallas_call(
        functools.partial(fetch_kernel, d0),
        out_shape=[jax.ShapeDtypeStruct((D_STEP, depth, cols // 2), bf16)] * 4,
        in_specs=[pl.BlockSpec(memory_space=pl.ANY)] * 2,
        out_specs=[vmem] * 4,
        scratch_shapes=[pltpu.VMEM((D_STEP, depth, cols), f32), pltpu.SemaphoreType.DMA((D_STEP,))],
        compiler_params=pltpu.CompilerParams(vmem_limit_bytes=SMALL_LIMIT),
        cost_estimate=pl.CostEstimate(flops=0, bytes_accessed=8 * D_STEP * depth * cols, transcendentals=0),
        name="fetch_integrals",
    )(turn, ladder_ints)


def closing_kernel(n, turn_ref, *refs):
    a_refs, (hi_ref, lo_ref, acc_ref, out_ref) = refs[:n], refs[n:]
    deep = D_STEP * LANES
    w_hi = hi_ref[...].reshape(deep, -1)
    w_lo = lo_ref[...].reshape(deep, -1)
    out_ref[...] = acc_ref[...] + dot_split(side_by_side(a_refs), w_hi, w_lo)


def cycle_kernel(owners, steps, *refs):
    a_refs, u_ref, (send_ref, keep_ref, acc_ref, flat_ref) = refs[:owners], refs[owners], refs[owners + 1 :]
    step = pl.program_id(0)

    @pl.when(step == 0)
    def _():
        acc_ref[...] = jnp.zeros_like(acc_ref)
        flat_ref[...] = jnp.zeros_like(flat_ref)

    u = u_ref[...]
    tiles = a_refs[0].shape[0]
    a = jnp.concatenate([jnp.concatenate([r[t] for t in range(tiles)], axis=1) for r in a_refs], axis=0)
    acc_ref[...] += dot_split(a, *split(u.reshape(u.shape[0] * u.shape[1], u.shape[2])))

    @pl.when(step == steps - 1)
    def _():
        window = acc_ref.shape[0] // owners
        for k in range(owners):
            for j in range(acc_ref.shape[1] // LANES):
                for a in range(window):
                    flat_ref[k * CYCLE_PAD + j : k * CYCLE_PAD + j + 1, a * LANES : (a + 1) * LANES] = acc_ref[
                        k * window + a : k * window + a + 1, j * LANES : (j + 1) * LANES
                    ]
        pair_halves(flat_ref, send_ref, keep_ref)


def cycle_product(own, arrived, cycle_ints):
    owners = len(arrived) + 1
    tiles, window, _ = own.shape
    ks, cs, cols = cycle_ints.shape
    kb = 8
    steps = ks // kb
    per_step = tiles // steps
    half = (owners * CYCLE_PAD, window * LANES // 2)
    return pl.pallas_call(
        functools.partial(cycle_kernel, owners, steps),
        out_shape=[sds(*half)] * 2,
        grid=(steps,),
        in_specs=[pl.BlockSpec((per_step, window, LANES), lambda i: (i, 0, 0))] * owners
        + [pl.BlockSpec((kb, cs, cols), lambda i: (i, 0, 0))],
        out_specs=[pl.BlockSpec(half, lambda i: (0, 0))] * 2,
        scratch_shapes=[
            pltpu.VMEM((owners * window, cols), f32),
            pltpu.VMEM((owners * CYCLE_PAD, window * LANES), f32),
        ],
        compiler_params=pltpu.CompilerParams(vmem_limit_bytes=VMEM_LIMIT),
        cost_estimate=pl.CostEstimate(
            flops=6 * owners * window * ks * cs * cols, bytes_accessed=4 * ks * cs * cols, transcendentals=0
        ),
        name="cycle_product",
    )(own, *arrived, cycle_ints)


def add_blocks_kernel(keep_ref, recv_ref, *outs):
    rows = outs[0].shape[0]
    for k, out in enumerate(outs):
        part = slice(k * rows, (k + 1) * rows)
        out[...] = keep_ref[part] + recv_ref[part]


def add_blocks(keep, recv, n):
    rows, cols = keep.shape
    return small(add_blocks_kernel, [sds(rows // n, cols)] * n, [keep, recv])


def place_kernel(owner_cols, *refs):
    blocks, out_ref = refs[:-1], refs[-1]
    owner = lax.axis_index("occ")
    for k, src in enumerate(blocks):
        offset = (owner ^ k) * owner_cols
        for j in range(owner_cols):
            out_ref[pl.ds(offset + j, 1), :] = src[j : j + 1, :]


def line_kernel(n, *refs):
    cycle_ref, terms, outs = refs[0], refs[1:n], refs[n:]
    z = lax.axis_index("sec") // 2
    for q, out in enumerate(outs):
        cols = block_of(z ^ q)
        total = terms[0][:, cols]
        for t in terms[1:]:
            total = total + t[:, cols]
        out[...] = 0.5 * total + cycle_ref[:, cols]


def setup_kernel(turn_ref, counts, occ, vir, occ_ref, vir_ref, pair_in, pair_ref, den_ref, live_ref):
    owner = lax.axis_index("occ")
    rows, cols = pair_in.shape
    pair_ref[...] = pair_in[...]
    column = jnp.broadcast_to(occ_ref[...], (cols, rows)).T
    vir_pairs = vir[lax.axis_index("sec")] + vir_ref[:, :cols]
    den_ref[...] = (occ[owner] + column) - vir_pairs
    row = lax.broadcasted_iota(jnp.int32, (rows, cols), 0)
    live_ref[...] = (row < counts[owner]).astype(f32)


def setup(turn, live_pairs, occ_energy, vir_energy, pair_ints):
    vmem, smem = pl.BlockSpec(memory_space=pltpu.VMEM), pl.BlockSpec(memory_space=pltpu.SMEM)
    return pl.pallas_call(
        setup_kernel,
        out_shape=[sds(*pair_ints.shape)] * 3,
        in_specs=[pl.BlockSpec(memory_space=pl.ANY)] + [smem] * 3 + [vmem] * 3,
        out_specs=[vmem] * 3,
        compiler_params=pltpu.CompilerParams(vmem_limit_bytes=SMALL_LIMIT),
        cost_estimate=pl.CostEstimate(flops=0, bytes_accessed=16 * pair_ints.size, transcendentals=0),
        name="setup",
    )(turn, live_pairs, occ_energy, vir_energy, occ_energy.reshape(1, -1), vir_energy.reshape(1, -1), pair_ints)


def final_kernel(*refs):
    *terms, pair_ref, den_ref, live_ref, out_ref = refs
    total = pair_ref[...]
    for t in terms:
        total = total + t[...]
    out_ref[...] = total / den_ref[...] * live_ref[...]


def streamed_parts(amplitudes, live_pairs, ladder_ints, cycle_ints, pair_ints, occ_energy, vir_energy):
    owners = lax.axis_size("occ")
    sections = lax.axis_size("sec")
    owner_index = lax.axis_index("occ")
    owner_rows = I_OWNER * OCCUPIED
    owner_cols = OCCUPIED // owners
    d_share = amplitudes.shape[2]
    ids = owner_index.reshape(1).astype(jnp.int32)
    flipped = amplitudes.transpose(0, 2, 1)

    def exchange(values):
        moved = {}
        for k in reversed(range(1, owners)):
            moved[k] = lax.ppermute(values[k - 1], "occ", [(o, o ^ k) for o in range(owners)])
        return [moved[k] for k in range(1, owners)]

    def swap_pair(value):
        return lax.ppermute(value, "sec", [(s, s ^ 1) for s in range(sections)])

    starts = [d_share * c // CHUNK_UNITS for c in CHUNKS]
    chunks = [(d0, d1 - d0) for d0, d1 in zip(starts, [*starts[1:], d_share])]
    arrived = []
    turn = ids
    for c, (d0, dn) in enumerate(chunks):
        pieces = slice_chunk(after(ids, turn), flipped, owners, d0, dn)
        arrived.append(exchange(pieces))
        turn = pieces[0]
        if c == 0:
            window = cycle_window(after(ids, turn), live_pairs, flipped, A_WINDOW)
            windows = exchange([window] * (owners - 1))
            turn = window

    send, keep = cycle_product(window, windows, cycle_ints)
    recv = swap_pair(send)
    own, *sends = add_blocks(keep, recv, owners)
    blocks = [own, *exchange(sends)]
    cycle = small(functools.partial(place_kernel, owner_cols), sds(owner_rows, own.shape[1]), blocks)

    parts = fetch_integrals(after(ids, own), ladder_ints, chunks[-1][0])
    pair, denominator, live_out = setup(after(ids, parts[0]), live_pairs, occ_energy, vir_energy, pair_ints)
    far = chunks[2][0]
    (acc,) = ladder_product(after(ids, pair), [[flipped]], ladder_ints, far, lanes=True)
    own_send, own_keep, acc = ladder_product(ids, arrived[:2], ladder_ints, 0, own=flipped, acc=acc)
    own_recv = swap_pair(own_send)
    far_send, far_keep = ladder_product(ids, arrived[2:-1], ladder_ints, far, acc=acc)

    def closing(turn, hi, lo, acc):
        operands = [turn, *arrived[-1], hi, lo, acc]
        return small(functools.partial(closing_kernel, len(arrived[-1])), sds(*acc.shape), operands)

    far_send = closing(ids, *parts[:2], far_send)
    far_recv = swap_pair(far_send)
    far_keep = closing(after(ids, far_send), *parts[2:], far_keep)
    sends = add_blocks(far_keep, far_recv, owners - 1)
    terms = [cycle, own_keep, own_recv, *exchange(sends)]
    lines = sections // 2
    pieces = small(functools.partial(line_kernel, len(terms)), [sds(owner_rows, LANES)] * lines, terms)
    recvs = [
        lax.ppermute(pieces[q], "sec", [(s, s ^ (2 * q)) for s in range(sections)]) for q in reversed(range(1, lines))
    ]

    operands = [pieces[0], *recvs, pair, denominator, live_out]
    return small(final_kernel, sds(*pair_ints.shape), operands)


def gathered(amplitudes, live_pairs, ladder_ints, cycle_ints, pair_ints, occ_energy, vir_energy):
    owners = lax.axis_size("occ")
    sections = lax.axis_size("sec")
    owner_index = lax.axis_index("occ")
    section = lax.axis_index("sec")
    owner_rows = I_OWNER * OCCUPIED
    window_rows = I_OWNER * owners
    owner_cols = OCCUPIED // owners
    col_share = A_WINDOW * B_WINDOW // sections
    d_share = amplitudes.shape[2]
    live_count = lax.dynamic_slice_in_dim(live_pairs, owner_index, 1)[0]
    local_rows = lax.broadcasted_iota(jnp.int32, (owner_rows, 1, 1), 0)
    live_rows = (local_rows < live_count).astype(jnp.float32)
    masked = amplitudes * live_rows
    flat_tiles = masked.reshape(owner_rows, owners, VIRTUAL // owners * d_share)
    regrouped = lax.all_to_all(flat_tiles, "occ", split_axis=1, concat_axis=0, tiled=True)
    pair_total = regrouped.shape[0]
    ladder_part = 0.5 * jnp.dot(
        regrouped.reshape(pair_total, -1),
        ladder_ints.reshape(-1, A_WINDOW * B_WINDOW),
        precision=highest,
        preferred_element_type=jnp.float32,
    )
    cycle_local = masked[:, :A_WINDOW, :].reshape(owner_rows, A_WINDOW * d_share)
    cycle_flat = lax.all_gather(cycle_local, "occ", axis=0, tiled=True)
    cycle_rows = cycle_flat.reshape(window_rows, OCCUPIED, A_WINDOW, d_share)
    cycle_part = jnp.einsum(
        "ikac,kcn->ian",
        cycle_rows,
        cycle_ints,
        precision=highest,
        preferred_element_type=jnp.float32,
    )
    cycle_part = (
        cycle_part.reshape(window_rows, A_WINDOW, owner_cols, B_WINDOW)
        .transpose(0, 2, 1, 3)
        .reshape(window_rows, owner_cols, A_WINDOW * B_WINDOW)
    )
    ladder_grid = ladder_part.reshape(window_rows, OCCUPIED, A_WINDOW * B_WINDOW)
    offset = owner_index * owner_cols
    current_part = lax.dynamic_slice_in_dim(ladder_grid, offset, owner_cols, 1)
    ladder_grid = lax.dynamic_update_slice_in_dim(ladder_grid, current_part + cycle_part, offset, 1)
    combined = ladder_grid.reshape(pair_total, A_WINDOW * B_WINDOW)
    first_sum = lax.psum_scatter(combined, "sec", scatter_dimension=1, tiled=True)
    summed = lax.psum_scatter(first_sum, "occ", scatter_dimension=0, tiled=True)
    residual = summed + pair_ints
    occ_rows = lax.dynamic_slice_in_dim(occ_energy, owner_index * I_OWNER, I_OWNER)
    pair_energy = (occ_rows[:, None] + occ_energy[None, :]).reshape(owner_rows, 1)
    vir_pairs = (vir_energy[:A_WINDOW, None] + vir_energy[None, :B_WINDOW]).reshape(
        A_WINDOW * B_WINDOW
    )
    vir_cols = lax.dynamic_slice_in_dim(vir_pairs, section * col_share, col_share)
    denominator = pair_energy - vir_cols[None, :]
    live_out = (lax.broadcasted_iota(jnp.int32, (owner_rows, 1), 0) < live_count).astype(
        jnp.float32
    )
    return residual / denominator * live_out


def power_of_two(n):
    return n & (n - 1) == 0


def streams(owners, sections):
    return (
        1 < owners
        and power_of_two(owners)
        and 2 < sections
        and power_of_two(sections)
        and VIRTUAL == owners * LANES
        and A_WINDOW * B_WINDOW == sections * LANES
        and B_WINDOW == LANES
        and OCCUPIED // owners <= CYCLE_PAD
        and A_WINDOW == D_STEP
        and LANES % (VIRTUAL // sections) == 0
        and sections // 2 == owners
        and VIRTUAL // sections % (D_STEP * CHUNK_UNITS) == 0
    )


def solution(mesh):
    in_specs = (
        P("occ", None, "sec"),
        P(),
        P("occ", "sec", None),
        P(None, "sec", "occ"),
        P("occ", "sec"),
        P(),
        P(),
    )
    out_specs = P("occ", "sec")
    if not streams(mesh.shape["occ"], mesh.shape["sec"]):
        return jax.shard_map(gathered, mesh=mesh, in_specs=in_specs, out_specs=out_specs, check_vma=False)
    return jax.shard_map(streamed_parts, mesh=mesh, in_specs=in_specs, out_specs=out_specs, check_vma=False)
```

```python
import functools

import jax
import jax.numpy as jnp
from jax import lax
from jax.experimental import pallas as pl
from jax.experimental.pallas import tpu as pltpu
from jax.sharding import PartitionSpec as P


OCCUPIED = 48
VIRTUAL = 512
A_WINDOW = 8
B_WINDOW = 128
I_OWNER = 1
LANES = 128
D_STEP = 8
CHUNK_UNITS = 8
CHUNKS = (0, 1, 5, 7)
CYCLE_PAD = 16


f32 = jnp.float32
bf16 = jnp.bfloat16
highest = lax.Precision.HIGHEST
VMEM_LIMIT = 48 * 1024 * 1024
SMALL_LIMIT = 24 * 1024 * 1024


def split(x):
    hi = x.astype(bf16)
    return hi, (x - hi.astype(f32)).astype(bf16)


def dot(a, b):
    return jnp.dot(a, b, preferred_element_type=f32)


def dot_split(a, w_hi, w_lo):
    rows = a.shape[0]
    a_hi, a_lo = split(a)
    both = dot(jnp.concatenate([a_hi, a_lo], axis=0), w_hi)
    return both[:rows] + both[rows:] + dot(a_hi, w_lo)


def sds(*shape):
    return jax.ShapeDtypeStruct(shape, f32)


def small(kernel, out_shape, operands, scratch=()):
    vmem = pl.BlockSpec(memory_space=pltpu.VMEM)
    outs = out_shape if isinstance(out_shape, list) else [out_shape]
    moved = 4 * sum(x.size for x in [*operands, *outs])
    return pl.pallas_call(
        kernel,
        out_shape=out_shape,
        in_specs=[vmem] * len(operands),
        out_specs=[vmem] * len(outs) if isinstance(out_shape, list) else vmem,
        scratch_shapes=list(scratch),
        compiler_params=pltpu.CompilerParams(vmem_limit_bytes=SMALL_LIMIT),
        cost_estimate=pl.CostEstimate(flops=0, bytes_accessed=moved, transcendentals=0),
    )(*operands)


def after(value, earlier):
    return lax.optimization_barrier((value, earlier))[0]


def block_of(index):
    return pl.ds(pl.multiple_of(index * LANES, LANES), LANES)


def slice_kernel(d0, turn_ref, a_ref, *refs):
    outs, sem = refs[:-1], refs[-1]
    owner = lax.axis_index("occ")
    copies = [
        pltpu.make_async_copy(a_ref.at[:, pl.ds(d0, out.shape[1]), block_of(owner ^ k)], out, sem.at[k - 1])
        for k, out in enumerate(outs, start=1)
    ]
    for copy in copies:
        copy.start()
    for copy in copies:
        copy.wait()


def slice_chunk(turn, flipped, owners, d0, dn):
    rows = flipped.shape[0]
    n = owners - 1
    return pl.pallas_call(
        functools.partial(slice_kernel, d0),
        out_shape=[sds(rows, dn, LANES)] * n,
        in_specs=[pl.BlockSpec(memory_space=pl.ANY)] * 2,
        out_specs=[pl.BlockSpec(memory_space=pltpu.VMEM)] * n,
        scratch_shapes=[pltpu.SemaphoreType.DMA((n,))],
        compiler_params=pltpu.CompilerParams(vmem_limit_bytes=VMEM_LIMIT),
        cost_estimate=pl.CostEstimate(flops=0, bytes_accessed=8 * n * rows * dn * LANES, transcendentals=0),
        name="slices",
    )(turn, flipped)


def window_kernel(turn_ref, counts, a_ref, out_ref, tile_ref, sem):
    parts, rows, depth, _ = tile_ref.shape
    copies = [
        pltpu.make_async_copy(a_ref.at[pl.ds(p * rows, rows), :, pl.ds(0, LANES)], tile_ref.at[p], sem.at[p])
        for p in range(parts)
    ]
    for copy in copies:
        copy.start()
    live = counts[lax.axis_index("occ")]
    window = out_ref.shape[1]
    per_tile = LANES // depth
    pair = lax.broadcasted_iota(jnp.int32, (window, LANES), 1) // depth
    for p, copy in enumerate(copies):
        copy.wait()
        for t in range(rows // per_tile):
            flat = tile_ref[p, pl.ds(t * per_tile, per_tile)].reshape(LANES, LANES)
            tile = p * (rows // per_tile) + t
            out_ref[tile] = jnp.where(pair + tile * per_tile < live, flat.T[:window], 0.0)


def cycle_window(turn, counts, flipped, window):
    rows, depth, _ = flipped.shape
    hbm = pl.BlockSpec(memory_space=pl.ANY)
    return pl.pallas_call(
        window_kernel,
        out_shape=sds(rows * depth // LANES, window, LANES),
        in_specs=[hbm, pl.BlockSpec(memory_space=pltpu.SMEM), hbm],
        out_specs=pl.BlockSpec(memory_space=pltpu.VMEM),
        scratch_shapes=[pltpu.VMEM((4, rows // 4, depth, LANES), f32), pltpu.SemaphoreType.DMA((4,))],
        compiler_params=pltpu.CompilerParams(vmem_limit_bytes=VMEM_LIMIT),
        cost_estimate=pl.CostEstimate(flops=0, bytes_accessed=4 * rows * depth * LANES, transcendentals=0),
        name="cycle_window",
    )(turn, counts, flipped)


def side_by_side(refs):
    return jnp.concatenate([jnp.concatenate([r[:, d, :] for d in range(D_STEP)], axis=1) for r in refs], axis=0)


def gather_copies(w_ref, buf_ref, sem, block, slot):
    return [
        pltpu.make_async_copy(w_ref.at[:, block * D_STEP + d, :], buf_ref.at[slot, d], sem.at[slot, d])
        for d in range(D_STEP)
    ]


def ladder_kernel(block0, steps, own, last, n, turn, *refs):
    own_refs, refs = refs[:own], refs[own:]
    groups = [refs[g * n : (g + 1) * n] for g in range(len(steps))]
    w_ref, rest = refs[len(steps) * n], refs[len(steps) * n + 1 :]
    buf_ref, sem = rest[-2:]
    acc_in, outs = rest[: 1 if own or last else 0], rest[1 if own or last else 0 : -2]
    acc_ref = outs[-1]
    own_rows = own_refs[0].shape[0] if own else 0
    step, count = pl.program_id(0), pl.num_programs(0)
    slot = lax.rem(step, 2)

    @pl.when(step == 0)
    def _():
        for copy in gather_copies(w_ref, buf_ref, sem, block0, 0):
            copy.start()
        if last:
            acc_ref[...] = acc_in[0][...]
        else:
            acc_ref[own_rows:] = jnp.zeros((acc_ref.shape[0] - own_rows, acc_ref.shape[1]), f32)
        if own:
            acc_ref[:own_rows] = acc_in[0][...]

    @pl.when(step + 1 < count)
    def _():
        for copy in gather_copies(w_ref, buf_ref, sem, block0 + step + 1, 1 - slot):
            copy.start()

    for copy in gather_copies(w_ref, buf_ref, sem, block0 + step, slot):
        copy.wait()

    a = side_by_side(groups[-1])
    bound = sum(steps)
    for g in reversed(range(len(steps) - 1)):
        bound -= steps[g + 1]
        a = jnp.where(step < bound, side_by_side(groups[g]), a)
    if own:
        a = jnp.concatenate([side_by_side(own_refs), a], axis=0)
    w = buf_ref[slot].reshape(D_STEP * LANES, -1)
    acc_ref[...] += dot_split(a, *split(w))

    @pl.when(step == count - 1)
    def _():
        if last:
            pair_halves(acc_ref, outs[0], outs[1])
        if own:
            pair_halves(acc_ref.at[pl.ds(0, own_rows)], outs[0], outs[1])
            outs[2][...] = acc_ref[own_rows:]


def pair_halves(src_ref, send_ref, keep_ref):
    core = lax.rem(lax.axis_index("sec"), 2)
    for z in range(send_ref.shape[1] // LANES):
        cols = slice(z * LANES, (z + 1) * LANES)
        send_ref[:, cols] = src_ref[:, block_of(2 * z + 1 - core)]
        keep_ref[:, cols] = src_ref[:, block_of(2 * z + core)]


def ladder_product(turn, groups, ladder_ints, d0, own=None, acc=None, lanes=False):
    n = len(groups[0])
    rows = groups[0][0].shape[0]
    depth, _, cols = ladder_ints.shape
    with_own, last = own is not None, own is None and acc is not None
    steps = [group[0].shape[1] // D_STEP for group in groups]
    block0 = d0 // D_STEP
    if lanes:
        steps = [steps[0] - block0]
    count = sum(steps)

    def total(rows, cols):
        return sds(rows, cols), pl.BlockSpec((rows, cols), lambda i, turn: (0, 0))

    def rows_spec(g):
        before = sum(steps[:g])
        return pl.BlockSpec((rows, D_STEP, LANES), lambda i, turn: (0, jnp.clip(i - before, 0, steps[g] - 1), 0))

    own_spec = pl.BlockSpec((rows, D_STEP, LANES), lambda i, turn: (0, block0 + i, turn[0]))
    if with_own:
        outs = [total(rows, cols // 2)] * 2 + [total(n * rows, cols)]
    else:
        outs = [total(n * rows, cols // 2)] * 2 if last else [total(n * rows, cols)]
    all_rows = (n + with_own) * rows
    return pl.pallas_call(
        functools.partial(ladder_kernel, block0, steps, with_own, last, n),
        out_shape=[shape for shape, _ in outs],
        grid_spec=pltpu.PrefetchScalarGridSpec(
            num_scalar_prefetch=1,
            grid=(count,),
            in_specs=[own_spec] * with_own
            + [own_spec if lanes else rows_spec(g) for g in range(len(groups)) for _ in range(n)]
            + [pl.BlockSpec(memory_space=pl.ANY)]
            + ([] if acc is None else [total(*acc.shape)[1]]),
            out_specs=[spec for _, spec in outs],
            scratch_shapes=([pltpu.VMEM((all_rows, cols), f32)] if with_own or last else [])
            + [pltpu.VMEM((2, D_STEP, depth, cols), f32), pltpu.SemaphoreType.DMA((2, D_STEP))],
        ),
        compiler_params=pltpu.CompilerParams(vmem_limit_bytes=VMEM_LIMIT),
        cost_estimate=pl.CostEstimate(
            flops=6 * all_rows * count * D_STEP * depth * cols,
            bytes_accessed=4 * count * D_STEP * depth * cols,
            transcendentals=0,
        ),
        name="ladder_product",
    )(
        turn,
        *([own] if with_own else []),
        *[value for group in groups for value in group],
        ladder_ints,
        *([] if acc is None else [acc]),
    )


def fetch_kernel(d0, turn_ref, w_ref, *refs):
    send_refs, keep_refs, (raw_ref, sem) = refs[:2], refs[2:4], refs[4:]
    copies = [
        pltpu.make_async_copy(w_ref.at[:, d0 + d, :], raw_ref.at[d], sem.at[d]) for d in range(raw_ref.shape[0])
    ]
    for copy in copies:
        copy.start()
    core = lax.rem(lax.axis_index("sec"), 2)
    for d, copy in enumerate(copies):
        copy.wait()
        for z in range(send_refs[0].shape[2] // LANES):
            cols = slice(z * LANES, (z + 1) * LANES)
            send_refs[0][d, :, cols], send_refs[1][d, :, cols] = split(raw_ref[d, :, block_of(2 * z + 1 - core)])
            keep_refs[0][d, :, cols], keep_refs[1][d, :, cols] = split(raw_ref[d, :, block_of(2 * z + core)])


def fetch_integrals(turn, ladder_ints, d0):
    depth, _, cols = ladder_ints.shape
    vmem = pl.BlockSpec(memory_space=pltpu.VMEM)
    return pl.pallas_call(
        functools.partial(fetch_kernel, d0),
        out_shape=[jax.ShapeDtypeStruct((D_STEP, depth, cols // 2), bf16)] * 4,
        in_specs=[pl.BlockSpec(memory_space=pl.ANY)] * 2,
        out_specs=[vmem] * 4,
        scratch_shapes=[pltpu.VMEM((D_STEP, depth, cols), f32), pltpu.SemaphoreType.DMA((D_STEP,))],
        compiler_params=pltpu.CompilerParams(vmem_limit_bytes=SMALL_LIMIT),
        cost_estimate=pl.CostEstimate(flops=0, bytes_accessed=8 * D_STEP * depth * cols, transcendentals=0),
        name="fetch_integrals",
    )(turn, ladder_ints)


def closing_kernel(n, turn_ref, *refs):
    a_refs, (hi_ref, lo_ref, acc_ref, out_ref) = refs[:n], refs[n:]
    deep = D_STEP * LANES
    w_hi = hi_ref[...].reshape(deep, -1)
    w_lo = lo_ref[...].reshape(deep, -1)
    out_ref[...] = acc_ref[...] + dot_split(side_by_side(a_refs), w_hi, w_lo)


def cycle_kernel(owners, steps, *refs):
    a_refs, u_ref, (send_ref, keep_ref, acc_ref, flat_ref) = refs[:owners], refs[owners], refs[owners + 1 :]
    step = pl.program_id(0)

    @pl.when(step == 0)
    def _():
        acc_ref[...] = jnp.zeros_like(acc_ref)
        flat_ref[...] = jnp.zeros_like(flat_ref)

    u = u_ref[...]
    tiles = a_refs[0].shape[0]
    a = jnp.concatenate([jnp.concatenate([r[t] for t in range(tiles)], axis=1) for r in a_refs], axis=0)
    acc_ref[...] += dot_split(a, *split(u.reshape(u.shape[0] * u.shape[1], u.shape[2])))

    @pl.when(step == steps - 1)
    def _():
        window = acc_ref.shape[0] // owners
        for k in range(owners):
            for j in range(acc_ref.shape[1] // LANES):
                for a in range(window):
                    flat_ref[k * CYCLE_PAD + j : k * CYCLE_PAD + j + 1, a * LANES : (a + 1) * LANES] = acc_ref[
                        k * window + a : k * window + a + 1, j * LANES : (j + 1) * LANES
                    ]
        pair_halves(flat_ref, send_ref, keep_ref)


def cycle_product(own, arrived, cycle_ints):
    owners = len(arrived) + 1
    tiles, window, _ = own.shape
    ks, cs, cols = cycle_ints.shape
    kb = 8
    steps = ks // kb
    per_step = tiles // steps
    half = (owners * CYCLE_PAD, window * LANES // 2)
    return pl.pallas_call(
        functools.partial(cycle_kernel, owners, steps),
        out_shape=[sds(*half)] * 2,
        grid=(steps,),
        in_specs=[pl.BlockSpec((per_step, window, LANES), lambda i: (i, 0, 0))] * owners
        + [pl.BlockSpec((kb, cs, cols), lambda i: (i, 0, 0))],
        out_specs=[pl.BlockSpec(half, lambda i: (0, 0))] * 2,
        scratch_shapes=[
            pltpu.VMEM((owners * window, cols), f32),
            pltpu.VMEM((owners * CYCLE_PAD, window * LANES), f32),
        ],
        compiler_params=pltpu.CompilerParams(vmem_limit_bytes=VMEM_LIMIT),
        cost_estimate=pl.CostEstimate(
            flops=6 * owners * window * ks * cs * cols, bytes_accessed=4 * ks * cs * cols, transcendentals=0
        ),
        name="cycle_product",
    )(own, *arrived, cycle_ints)


def add_blocks_kernel(keep_ref, recv_ref, *outs):
    rows = outs[0].shape[0]
    for k, out in enumerate(outs):
        part = slice(k * rows, (k + 1) * rows)
        out[...] = keep_ref[part] + recv_ref[part]


def add_blocks(keep, recv, n):
    rows, cols = keep.shape
    return small(add_blocks_kernel, [sds(rows // n, cols)] * n, [keep, recv])


def place_kernel(owner_cols, *refs):
    blocks, out_ref = refs[:-1], refs[-1]
    owner = lax.axis_index("occ")
    for k, src in enumerate(blocks):
        offset = (owner ^ k) * owner_cols
        for j in range(owner_cols):
            out_ref[pl.ds(offset + j, 1), :] = src[j : j + 1, :]


def pair_pieces_kernel(n, keep_ref, recv_ref, *outs):
    z = lax.axis_index("sec") // 2
    rows = outs[0].shape[0]
    per_half = outs[0].shape[1] // LANES
    for h in range(2):
        for k in range(n):
            part = slice(k * rows, (k + 1) * rows)
            for t in range(per_half):
                cols = block_of(z ^ (2 * per_half - 1 - h * per_half - t))
                outs[h * n + k][:, t * LANES : (t + 1) * LANES] = keep_ref[part, cols] + recv_ref[part, cols]


def line_kernel(n, lines, cycle_ref, keep_ref, recv_ref, *refs):
    terms, outs = refs[:n], refs[n:]
    z = lax.axis_index("sec") // 2
    for t, (q, out) in enumerate(zip(lines, outs)):
        cols = block_of(z ^ q)
        total = keep_ref[:, cols] + recv_ref[:, cols]
        for term in terms:
            total = total + term[:, t * LANES : (t + 1) * LANES]
        out[...] = 0.5 * total + cycle_ref[:, cols]


def final_kernel(*refs):
    *terms, pair_ref, den_ref, live_ref, out_ref = refs
    total = pair_ref[...]
    for t in terms:
        total = total + t[...]
    out_ref[...] = total / den_ref[...] * live_ref[...]


def setup_kernel(turn_ref, counts, occ, vir, occ_ref, vir_ref, pair_in, pair_ref, den_ref, live_ref):
    owner = lax.axis_index("occ")
    rows, cols = pair_in.shape
    pair_ref[...] = pair_in[...]
    column = jnp.broadcast_to(occ_ref[...], (cols, rows)).T
    vir_pairs = vir[lax.axis_index("sec")] + vir_ref[:, :cols]
    den_ref[...] = (occ[owner] + column) - vir_pairs
    row = lax.broadcasted_iota(jnp.int32, (rows, cols), 0)
    live_ref[...] = (row < counts[owner]).astype(f32)


def setup(turn, live_pairs, occ_energy, vir_energy, pair_ints):
    vmem, smem = pl.BlockSpec(memory_space=pltpu.VMEM), pl.BlockSpec(memory_space=pltpu.SMEM)
    return pl.pallas_call(
        setup_kernel,
        out_shape=[sds(*pair_ints.shape)] * 3,
        in_specs=[pl.BlockSpec(memory_space=pl.ANY)] + [smem] * 3 + [vmem] * 3,
        out_specs=[vmem] * 3,
        compiler_params=pltpu.CompilerParams(vmem_limit_bytes=SMALL_LIMIT),
        cost_estimate=pl.CostEstimate(flops=0, bytes_accessed=16 * pair_ints.size, transcendentals=0),
        name="setup",
    )(turn, live_pairs, occ_energy, vir_energy, occ_energy.reshape(1, -1), vir_energy.reshape(1, -1), pair_ints)


def final_kernel(*refs):
    *terms, pair_ref, den_ref, live_ref, out_ref = refs
    total = pair_ref[...]
    for t in terms:
        total = total + t[...]
    out_ref[...] = total / den_ref[...] * live_ref[...]


def streamed_parts(amplitudes, live_pairs, ladder_ints, cycle_ints, pair_ints, occ_energy, vir_energy):
    owners = lax.axis_size("occ")
    sections = lax.axis_size("sec")
    owner_index = lax.axis_index("occ")
    owner_rows = I_OWNER * OCCUPIED
    owner_cols = OCCUPIED // owners
    d_share = amplitudes.shape[2]
    ids = owner_index.reshape(1).astype(jnp.int32)
    flipped = amplitudes.transpose(0, 2, 1)

    def exchange(values):
        moved = {}
        for k in reversed(range(1, owners)):
            moved[k] = lax.ppermute(values[k - 1], "occ", [(o, o ^ k) for o in range(owners)])
        return [moved[k] for k in range(1, owners)]

    def swap_pair(value):
        return lax.ppermute(value, "sec", [(s, s ^ 1) for s in range(sections)])

    starts = [d_share * c // CHUNK_UNITS for c in CHUNKS]
    chunks = [(d0, d1 - d0) for d0, d1 in zip(starts, [*starts[1:], d_share])]
    arrived = []
    turn = ids
    for c, (d0, dn) in enumerate(chunks):
        pieces = slice_chunk(after(ids, turn), flipped, owners, d0, dn)
        arrived.append(exchange(pieces))
        turn = pieces[0]
        if c == 0:
            window = cycle_window(after(ids, turn), live_pairs, flipped, A_WINDOW)
            windows = exchange([window] * (owners - 1))
            turn = window

    send, keep = cycle_product(window, windows, cycle_ints)
    recv = swap_pair(send)
    own, *sends = add_blocks(keep, recv, owners)
    blocks = [own, *exchange(sends)]
    cycle = small(functools.partial(place_kernel, owner_cols), sds(owner_rows, own.shape[1]), blocks)

    parts = fetch_integrals(after(ids, own), ladder_ints, chunks[-1][0])
    pair, denominator, live_out = setup(after(ids, parts[0]), live_pairs, occ_energy, vir_energy, pair_ints)
    far = chunks[2][0]
    (acc,) = ladder_product(after(ids, pair), [[flipped]], ladder_ints, far, lanes=True)
    own_send, own_keep, acc = ladder_product(ids, arrived[:2], ladder_ints, 0, own=flipped, acc=acc)
    own_recv = swap_pair(own_send)
    far_send, far_keep = ladder_product(ids, arrived[2:-1], ladder_ints, far, acc=acc)

    def closing(turn, hi, lo, acc):
        operands = [turn, *arrived[-1], hi, lo, acc]
        return small(functools.partial(closing_kernel, len(arrived[-1])), sds(*acc.shape), operands)

    far_send = closing(ids, *parts[:2], far_send)
    far_recv = swap_pair(far_send)
    far_keep = closing(after(ids, far_send), *parts[2:], far_keep)
    lines = sections // 2
    n = owners - 1
    sends = small(
        functools.partial(pair_pieces_kernel, n), [sds(owner_rows, lines // 2 * LANES)] * (2 * n), [far_keep, far_recv]
    )
    far_terms = exchange(sends[:n])
    near_terms = exchange(sends[n:])
    order = list(reversed(range(lines)))

    def line(distances, terms):
        return small(
            functools.partial(line_kernel, n, distances),
            [sds(owner_rows, LANES)] * len(distances),
            [cycle, own_keep, own_recv, *terms],
        )

    def along(distances, pieces):
        return [
            lax.ppermute(piece, "sec", [(s, s ^ (2 * q)) for s in range(sections)])
            for q, piece in zip(distances, pieces)
        ]

    pieces = line(order[: lines // 2], far_terms)
    recvs = along(order, pieces)
    *pieces, own_piece = line(order[lines // 2 :], near_terms)
    recvs += along(order[lines // 2 :], pieces)

    operands = [own_piece, *recvs, pair, denominator, live_out]
    return small(final_kernel, sds(*pair_ints.shape), operands)


def gathered(amplitudes, live_pairs, ladder_ints, cycle_ints, pair_ints, occ_energy, vir_energy):
    owners = lax.axis_size("occ")
    sections = lax.axis_size("sec")
    owner_index = lax.axis_index("occ")
    section = lax.axis_index("sec")
    owner_rows = I_OWNER * OCCUPIED
    window_rows = I_OWNER * owners
    owner_cols = OCCUPIED // owners
    col_share = A_WINDOW * B_WINDOW // sections
    d_share = amplitudes.shape[2]
    live_count = lax.dynamic_slice_in_dim(live_pairs, owner_index, 1)[0]
    local_rows = lax.broadcasted_iota(jnp.int32, (owner_rows, 1, 1), 0)
    live_rows = (local_rows < live_count).astype(jnp.float32)
    masked = amplitudes * live_rows
    flat_tiles = masked.reshape(owner_rows, owners, VIRTUAL // owners * d_share)
    regrouped = lax.all_to_all(flat_tiles, "occ", split_axis=1, concat_axis=0, tiled=True)
    pair_total = regrouped.shape[0]
    ladder_part = 0.5 * jnp.dot(
        regrouped.reshape(pair_total, -1),
        ladder_ints.reshape(-1, A_WINDOW * B_WINDOW),
        precision=highest,
        preferred_element_type=jnp.float32,
    )
    cycle_local = masked[:, :A_WINDOW, :].reshape(owner_rows, A_WINDOW * d_share)
    cycle_flat = lax.all_gather(cycle_local, "occ", axis=0, tiled=True)
    cycle_rows = cycle_flat.reshape(window_rows, OCCUPIED, A_WINDOW, d_share)
    cycle_part = jnp.einsum(
        "ikac,kcn->ian",
        cycle_rows,
        cycle_ints,
        precision=highest,
        preferred_element_type=jnp.float32,
    )
    cycle_part = (
        cycle_part.reshape(window_rows, A_WINDOW, owner_cols, B_WINDOW)
        .transpose(0, 2, 1, 3)
        .reshape(window_rows, owner_cols, A_WINDOW * B_WINDOW)
    )
    ladder_grid = ladder_part.reshape(window_rows, OCCUPIED, A_WINDOW * B_WINDOW)
    offset = owner_index * owner_cols
    current_part = lax.dynamic_slice_in_dim(ladder_grid, offset, owner_cols, 1)
    ladder_grid = lax.dynamic_update_slice_in_dim(ladder_grid, current_part + cycle_part, offset, 1)
    combined = ladder_grid.reshape(pair_total, A_WINDOW * B_WINDOW)
    first_sum = lax.psum_scatter(combined, "sec", scatter_dimension=1, tiled=True)
    summed = lax.psum_scatter(first_sum, "occ", scatter_dimension=0, tiled=True)
    residual = summed + pair_ints
    occ_rows = lax.dynamic_slice_in_dim(occ_energy, owner_index * I_OWNER, I_OWNER)
    pair_energy = (occ_rows[:, None] + occ_energy[None, :]).reshape(owner_rows, 1)
    vir_pairs = (vir_energy[:A_WINDOW, None] + vir_energy[None, :B_WINDOW]).reshape(
        A_WINDOW * B_WINDOW
    )
    vir_cols = lax.dynamic_slice_in_dim(vir_pairs, section * col_share, col_share)
    denominator = pair_energy - vir_cols[None, :]
    live_out = (lax.broadcasted_iota(jnp.int32, (owner_rows, 1), 0) < live_count).astype(
        jnp.float32
    )
    return residual / denominator * live_out


def power_of_two(n):
    return n & (n - 1) == 0


def streams(owners, sections):
    return (
        1 < owners
        and power_of_two(owners)
        and 2 < sections
        and power_of_two(sections)
        and VIRTUAL == owners * LANES
        and A_WINDOW * B_WINDOW == sections * LANES
        and B_WINDOW == LANES
        and OCCUPIED // owners <= CYCLE_PAD
        and A_WINDOW == D_STEP
        and LANES % (VIRTUAL // sections) == 0
        and sections // 2 == owners
        and VIRTUAL // sections % (D_STEP * CHUNK_UNITS) == 0
    )


def solution(mesh):
    in_specs = (
        P("occ", None, "sec"),
        P(),
        P("occ", "sec", None),
        P(None, "sec", "occ"),
        P("occ", "sec"),
        P(),
        P(),
    )
    out_specs = P("occ", "sec")
    if not streams(mesh.shape["occ"], mesh.shape["sec"]):
        return jax.shard_map(gathered, mesh=mesh, in_specs=in_specs, out_specs=out_specs, check_vma=False)
    return jax.shard_map(streamed_parts, mesh=mesh, in_specs=in_specs, out_specs=out_specs, check_vma=False)
```

```python
import functools

import jax
import jax.numpy as jnp
from jax import lax
from jax.experimental import pallas as pl
from jax.experimental.pallas import tpu as pltpu
from jax.sharding import PartitionSpec as P


OCCUPIED = 48
VIRTUAL = 512
A_WINDOW = 8
B_WINDOW = 128
I_OWNER = 1
LANES = 128
D_STEP = 8
CHUNK_UNITS = 8
CHUNKS = (0, 1, 5, 7)
CYCLE_PAD = 16


f32 = jnp.float32
bf16 = jnp.bfloat16
highest = lax.Precision.HIGHEST
VMEM_LIMIT = 48 * 1024 * 1024
SMALL_LIMIT = 24 * 1024 * 1024


def split(x):
    hi = x.astype(bf16)
    return hi, (x - hi.astype(f32)).astype(bf16)


def dot(a, b):
    return jnp.dot(a, b, preferred_element_type=f32)


def dot_split(a, w_hi, w_lo):
    rows = a.shape[0]
    a_hi, a_lo = split(a)
    both = dot(jnp.concatenate([a_hi, a_lo], axis=0), w_hi)
    return both[:rows] + both[rows:] + dot(a_hi, w_lo)


def sds(*shape):
    return jax.ShapeDtypeStruct(shape, f32)


def small(kernel, out_shape, operands, scratch=()):
    vmem = pl.BlockSpec(memory_space=pltpu.VMEM)
    outs = out_shape if isinstance(out_shape, list) else [out_shape]
    moved = 4 * sum(x.size for x in [*operands, *outs])
    return pl.pallas_call(
        kernel,
        out_shape=out_shape,
        in_specs=[vmem] * len(operands),
        out_specs=[vmem] * len(outs) if isinstance(out_shape, list) else vmem,
        scratch_shapes=list(scratch),
        compiler_params=pltpu.CompilerParams(vmem_limit_bytes=SMALL_LIMIT),
        cost_estimate=pl.CostEstimate(flops=0, bytes_accessed=moved, transcendentals=0),
    )(*operands)


def after(value, earlier):
    return lax.optimization_barrier((value, earlier))[0]


def block_of(index):
    return pl.ds(pl.multiple_of(index * LANES, LANES), LANES)


def slice_kernel(d0, turn_ref, a_ref, *refs):
    outs, sem = refs[:-1], refs[-1]
    owner = lax.axis_index("occ")
    copies = [
        pltpu.make_async_copy(a_ref.at[:, pl.ds(d0, out.shape[1]), block_of(owner ^ k)], out, sem.at[k - 1])
        for k, out in enumerate(outs, start=1)
    ]
    for copy in copies:
        copy.start()
    for copy in copies:
        copy.wait()


def slice_chunk(turn, flipped, owners, d0, dn):
    rows = flipped.shape[0]
    n = owners - 1
    return pl.pallas_call(
        functools.partial(slice_kernel, d0),
        out_shape=[sds(rows, dn, LANES)] * n,
        in_specs=[pl.BlockSpec(memory_space=pl.ANY)] * 2,
        out_specs=[pl.BlockSpec(memory_space=pltpu.VMEM)] * n,
        scratch_shapes=[pltpu.SemaphoreType.DMA((n,))],
        compiler_params=pltpu.CompilerParams(vmem_limit_bytes=VMEM_LIMIT),
        cost_estimate=pl.CostEstimate(flops=0, bytes_accessed=8 * n * rows * dn * LANES, transcendentals=0),
        name="slices",
    )(turn, flipped)


def window_kernel(turn_ref, counts, a_ref, out_ref, tile_ref, sem):
    parts, rows, depth, _ = tile_ref.shape
    copies = [
        pltpu.make_async_copy(a_ref.at[pl.ds(p * rows, rows), :, pl.ds(0, LANES)], tile_ref.at[p], sem.at[p])
        for p in range(parts)
    ]
    for copy in copies:
        copy.start()
    live = counts[lax.axis_index("occ")]
    window = out_ref.shape[1]
    per_tile = LANES // depth
    pair = lax.broadcasted_iota(jnp.int32, (window, LANES), 1) // depth
    for p, copy in enumerate(copies):
        copy.wait()
        for t in range(rows // per_tile):
            flat = tile_ref[p, pl.ds(t * per_tile, per_tile)].reshape(LANES, LANES)
            tile = p * (rows // per_tile) + t
            out_ref[tile] = jnp.where(pair + tile * per_tile < live, flat.T[:window], 0.0)


def cycle_window(turn, counts, flipped, window):
    rows, depth, _ = flipped.shape
    hbm = pl.BlockSpec(memory_space=pl.ANY)
    return pl.pallas_call(
        window_kernel,
        out_shape=sds(rows * depth // LANES, window, LANES),
        in_specs=[hbm, pl.BlockSpec(memory_space=pltpu.SMEM), hbm],
        out_specs=pl.BlockSpec(memory_space=pltpu.VMEM),
        scratch_shapes=[pltpu.VMEM((4, rows // 4, depth, LANES), f32), pltpu.SemaphoreType.DMA((4,))],
        compiler_params=pltpu.CompilerParams(vmem_limit_bytes=VMEM_LIMIT),
        cost_estimate=pl.CostEstimate(flops=0, bytes_accessed=4 * rows * depth * LANES, transcendentals=0),
        name="cycle_window",
    )(turn, counts, flipped)


def side_by_side(refs):
    return jnp.concatenate([jnp.concatenate([r[:, d, :] for d in range(D_STEP)], axis=1) for r in refs], axis=0)


def gather_copies(w_ref, buf_ref, sem, block, slot):
    return [
        pltpu.make_async_copy(w_ref.at[:, block * D_STEP + d, :], buf_ref.at[slot, d], sem.at[slot, d])
        for d in range(D_STEP)
    ]


def ladder_kernel(block0, steps, own, last, n, turn, *refs):
    own_refs, refs = refs[:own], refs[own:]
    groups = [refs[g * n : (g + 1) * n] for g in range(len(steps))]
    w_ref, rest = refs[len(steps) * n], refs[len(steps) * n + 1 :]
    buf_ref, sem = rest[-2:]
    acc_in, outs = rest[: 1 if own or last else 0], rest[1 if own or last else 0 : -2]
    acc_ref = outs[-1]
    own_rows = own_refs[0].shape[0] if own else 0
    step, count = pl.program_id(0), pl.num_programs(0)
    slot = lax.rem(step, 2)

    @pl.when(step == 0)
    def _():
        for copy in gather_copies(w_ref, buf_ref, sem, block0, 0):
            copy.start()
        if last:
            acc_ref[...] = acc_in[0][...]
        else:
            acc_ref[own_rows:] = jnp.zeros((acc_ref.shape[0] - own_rows, acc_ref.shape[1]), f32)
        if own:
            acc_ref[:own_rows] = acc_in[0][...]

    @pl.when(step + 1 < count)
    def _():
        for copy in gather_copies(w_ref, buf_ref, sem, block0 + step + 1, 1 - slot):
            copy.start()

    for copy in gather_copies(w_ref, buf_ref, sem, block0 + step, slot):
        copy.wait()

    a = side_by_side(groups[-1])
    bound = sum(steps)
    for g in reversed(range(len(steps) - 1)):
        bound -= steps[g + 1]
        a = jnp.where(step < bound, side_by_side(groups[g]), a)
    if own:
        a = jnp.concatenate([side_by_side(own_refs), a], axis=0)
    w = buf_ref[slot].reshape(D_STEP * LANES, -1)
    acc_ref[...] += dot_split(a, *split(w))

    @pl.when(step == count - 1)
    def _():
        if last:
            pair_halves(acc_ref, outs[0], outs[1])
        if own:
            pair_halves(acc_ref.at[pl.ds(0, own_rows)], outs[0], outs[1])
            outs[2][...] = acc_ref[own_rows:]


def pair_halves(src_ref, send_ref, keep_ref):
    core = lax.rem(lax.axis_index("sec"), 2)
    for z in range(send_ref.shape[1] // LANES):
        cols = slice(z * LANES, (z + 1) * LANES)
        send_ref[:, cols] = src_ref[:, block_of(2 * z + 1 - core)]
        keep_ref[:, cols] = src_ref[:, block_of(2 * z + core)]


def ladder_product(turn, groups, ladder_ints, d0, own=None, acc=None, lanes=False):
    n = len(groups[0])
    rows = groups[0][0].shape[0]
    depth, _, cols = ladder_ints.shape
    with_own, last = own is not None, own is None and acc is not None
    steps = [group[0].shape[1] // D_STEP for group in groups]
    block0 = d0 // D_STEP
    if lanes:
        steps = [steps[0] - block0]
    count = sum(steps)

    def total(rows, cols):
        return sds(rows, cols), pl.BlockSpec((rows, cols), lambda i, turn: (0, 0))

    def rows_spec(g):
        before = sum(steps[:g])
        return pl.BlockSpec((rows, D_STEP, LANES), lambda i, turn: (0, jnp.clip(i - before, 0, steps[g] - 1), 0))

    own_spec = pl.BlockSpec((rows, D_STEP, LANES), lambda i, turn: (0, block0 + i, turn[0]))
    if with_own:
        outs = [total(rows, cols // 2)] * 2 + [total(n * rows, cols)]
    else:
        outs = [total(n * rows, cols // 2)] * 2 if last else [total(n * rows, cols)]
    all_rows = (n + with_own) * rows
    return pl.pallas_call(
        functools.partial(ladder_kernel, block0, steps, with_own, last, n),
        out_shape=[shape for shape, _ in outs],
        grid_spec=pltpu.PrefetchScalarGridSpec(
            num_scalar_prefetch=1,
            grid=(count,),
            in_specs=[own_spec] * with_own
            + [own_spec if lanes else rows_spec(g) for g in range(len(groups)) for _ in range(n)]
            + [pl.BlockSpec(memory_space=pl.ANY)]
            + ([] if acc is None else [total(*acc.shape)[1]]),
            out_specs=[spec for _, spec in outs],
            scratch_shapes=([pltpu.VMEM((all_rows, cols), f32)] if with_own or last else [])
            + [pltpu.VMEM((2, D_STEP, depth, cols), f32), pltpu.SemaphoreType.DMA((2, D_STEP))],
        ),
        compiler_params=pltpu.CompilerParams(vmem_limit_bytes=VMEM_LIMIT),
        cost_estimate=pl.CostEstimate(
            flops=6 * all_rows * count * D_STEP * depth * cols,
            bytes_accessed=4 * count * D_STEP * depth * cols,
            transcendentals=0,
        ),
        name="ladder_product",
    )(
        turn,
        *([own] if with_own else []),
        *[value for group in groups for value in group],
        ladder_ints,
        *([] if acc is None else [acc]),
    )


def fetch_kernel(d0, turn_ref, w_ref, *refs):
    send_refs, keep_refs, (raw_ref, sem) = refs[:2], refs[2:4], refs[4:]
    copies = [
        pltpu.make_async_copy(w_ref.at[:, d0 + d, :], raw_ref.at[d], sem.at[d]) for d in range(raw_ref.shape[0])
    ]
    for copy in copies:
        copy.start()
    core = lax.rem(lax.axis_index("sec"), 2)
    for d, copy in enumerate(copies):
        copy.wait()
        for z in range(send_refs[0].shape[2] // LANES):
            cols = slice(z * LANES, (z + 1) * LANES)
            send_refs[0][d, :, cols], send_refs[1][d, :, cols] = split(raw_ref[d, :, block_of(2 * z + 1 - core)])
            keep_refs[0][d, :, cols], keep_refs[1][d, :, cols] = split(raw_ref[d, :, block_of(2 * z + core)])


def fetch_integrals(turn, ladder_ints, d0):
    depth, _, cols = ladder_ints.shape
    vmem = pl.BlockSpec(memory_space=pltpu.VMEM)
    return pl.pallas_call(
        functools.partial(fetch_kernel, d0),
        out_shape=[jax.ShapeDtypeStruct((D_STEP, depth, cols // 2), bf16)] * 4,
        in_specs=[pl.BlockSpec(memory_space=pl.ANY)] * 2,
        out_specs=[vmem] * 4,
        scratch_shapes=[pltpu.VMEM((D_STEP, depth, cols), f32), pltpu.SemaphoreType.DMA((D_STEP,))],
        compiler_params=pltpu.CompilerParams(vmem_limit_bytes=SMALL_LIMIT),
        cost_estimate=pl.CostEstimate(flops=0, bytes_accessed=8 * D_STEP * depth * cols, transcendentals=0),
        name="fetch_integrals",
    )(turn, ladder_ints)


def closing_kernel(n, turn_ref, *refs):
    a_refs, (hi_ref, lo_ref, acc_ref, out_ref) = refs[:n], refs[n:]
    deep = D_STEP * LANES
    w_hi = hi_ref[...].reshape(deep, -1)
    w_lo = lo_ref[...].reshape(deep, -1)
    out_ref[...] = acc_ref[...] + dot_split(side_by_side(a_refs), w_hi, w_lo)


def cycle_kernel(owners, steps, *refs):
    a_refs, u_ref, (send_ref, keep_ref, acc_ref, flat_ref) = refs[:owners], refs[owners], refs[owners + 1 :]
    step = pl.program_id(0)

    @pl.when(step == 0)
    def _():
        acc_ref[...] = jnp.zeros_like(acc_ref)
        flat_ref[...] = jnp.zeros_like(flat_ref)

    u = u_ref[...]
    tiles = a_refs[0].shape[0]
    a = jnp.concatenate([jnp.concatenate([r[t] for t in range(tiles)], axis=1) for r in a_refs], axis=0)
    acc_ref[...] += dot_split(a, *split(u.reshape(u.shape[0] * u.shape[1], u.shape[2])))

    @pl.when(step == steps - 1)
    def _():
        window = acc_ref.shape[0] // owners
        for k in range(owners):
            for j in range(acc_ref.shape[1] // LANES):
                for a in range(window):
                    flat_ref[k * CYCLE_PAD + j : k * CYCLE_PAD + j + 1, a * LANES : (a + 1) * LANES] = acc_ref[
                        k * window + a : k * window + a + 1, j * LANES : (j + 1) * LANES
                    ]
        pair_halves(flat_ref, send_ref, keep_ref)


def cycle_product(own, arrived, cycle_ints):
    owners = len(arrived) + 1
    tiles, window, _ = own.shape
    ks, cs, cols = cycle_ints.shape
    kb = 8
    steps = ks // kb
    per_step = tiles // steps
    half = (owners * CYCLE_PAD, window * LANES // 2)
    return pl.pallas_call(
        functools.partial(cycle_kernel, owners, steps),
        out_shape=[sds(*half)] * 2,
        grid=(steps,),
        in_specs=[pl.BlockSpec((per_step, window, LANES), lambda i: (i, 0, 0))] * owners
        + [pl.BlockSpec((kb, cs, cols), lambda i: (i, 0, 0))],
        out_specs=[pl.BlockSpec(half, lambda i: (0, 0))] * 2,
        scratch_shapes=[
            pltpu.VMEM((owners * window, cols), f32),
            pltpu.VMEM((owners * CYCLE_PAD, window * LANES), f32),
        ],
        compiler_params=pltpu.CompilerParams(vmem_limit_bytes=VMEM_LIMIT),
        cost_estimate=pl.CostEstimate(
            flops=6 * owners * window * ks * cs * cols, bytes_accessed=4 * ks * cs * cols, transcendentals=0
        ),
        name="cycle_product",
    )(own, *arrived, cycle_ints)


def add_blocks_kernel(keep_ref, recv_ref, *outs):
    rows = outs[0].shape[0]
    for k, out in enumerate(outs):
        part = slice(k * rows, (k + 1) * rows)
        out[...] = keep_ref[part] + recv_ref[part]


def add_blocks(keep, recv, n):
    rows, cols = keep.shape
    return small(add_blocks_kernel, [sds(rows // n, cols)] * n, [keep, recv])


def place_kernel(owner_cols, *refs):
    blocks, out_ref = refs[:-1], refs[-1]
    owner = lax.axis_index("occ")
    for k, src in enumerate(blocks):
        offset = (owner ^ k) * owner_cols
        for j in range(owner_cols):
            out_ref[pl.ds(offset + j, 1), :] = src[j : j + 1, :]


def pair_pieces_kernel(n, keep_ref, recv_ref, *outs):
    z = lax.axis_index("sec") // 2
    rows = outs[0].shape[0]
    others = outs[0].shape[1] // LANES
    for k in range(n):
        part = slice(k * rows, (k + 1) * rows)
        for t in range(others + 1):
            cols = block_of(z ^ (others - t))
            out, tile = (outs[k], t) if t < others else (outs[n + k], 0)
            out[:, tile * LANES : (tile + 1) * LANES] = keep_ref[part, cols] + recv_ref[part, cols]


def line_kernel(n, lines, cycle_ref, keep_ref, recv_ref, *refs):
    terms, outs = refs[:n], refs[n:]
    z = lax.axis_index("sec") // 2
    for t, (q, out) in enumerate(zip(lines, outs)):
        cols = block_of(z ^ q)
        total = keep_ref[:, cols] + recv_ref[:, cols]
        for term in terms:
            total = total + term[:, t * LANES : (t + 1) * LANES]
        out[...] = 0.5 * total + cycle_ref[:, cols]


def final_kernel(*refs):
    *terms, pair_ref, den_ref, live_ref, out_ref = refs
    total = pair_ref[...]
    for t in terms:
        total = total + t[...]
    out_ref[...] = total / den_ref[...] * live_ref[...]


def setup_kernel(turn_ref, counts, occ, vir, occ_ref, vir_ref, pair_in, pair_ref, den_ref, live_ref):
    owner = lax.axis_index("occ")
    rows, cols = pair_in.shape
    pair_ref[...] = pair_in[...]
    column = jnp.broadcast_to(occ_ref[...], (cols, rows)).T
    vir_pairs = vir[lax.axis_index("sec")] + vir_ref[:, :cols]
    den_ref[...] = (occ[owner] + column) - vir_pairs
    row = lax.broadcasted_iota(jnp.int32, (rows, cols), 0)
    live_ref[...] = (row < counts[owner]).astype(f32)


def setup(turn, live_pairs, occ_energy, vir_energy, pair_ints):
    vmem, smem = pl.BlockSpec(memory_space=pltpu.VMEM), pl.BlockSpec(memory_space=pltpu.SMEM)
    return pl.pallas_call(
        setup_kernel,
        out_shape=[sds(*pair_ints.shape)] * 3,
        in_specs=[pl.BlockSpec(memory_space=pl.ANY)] + [smem] * 3 + [vmem] * 3,
        out_specs=[vmem] * 3,
        compiler_params=pltpu.CompilerParams(vmem_limit_bytes=SMALL_LIMIT),
        cost_estimate=pl.CostEstimate(flops=0, bytes_accessed=16 * pair_ints.size, transcendentals=0),
        name="setup",
    )(turn, live_pairs, occ_energy, vir_energy, occ_energy.reshape(1, -1), vir_energy.reshape(1, -1), pair_ints)


def final_kernel(*refs):
    *terms, pair_ref, den_ref, live_ref, out_ref = refs
    total = pair_ref[...]
    for t in terms:
        total = total + t[...]
    out_ref[...] = total / den_ref[...] * live_ref[...]


def streamed_parts(amplitudes, live_pairs, ladder_ints, cycle_ints, pair_ints, occ_energy, vir_energy):
    owners = lax.axis_size("occ")
    sections = lax.axis_size("sec")
    owner_index = lax.axis_index("occ")
    owner_rows = I_OWNER * OCCUPIED
    owner_cols = OCCUPIED // owners
    d_share = amplitudes.shape[2]
    ids = owner_index.reshape(1).astype(jnp.int32)
    flipped = amplitudes.transpose(0, 2, 1)

    def exchange(values):
        moved = {}
        for k in reversed(range(1, owners)):
            moved[k] = lax.ppermute(values[k - 1], "occ", [(o, o ^ k) for o in range(owners)])
        return [moved[k] for k in range(1, owners)]

    def swap_pair(value):
        return lax.ppermute(value, "sec", [(s, s ^ 1) for s in range(sections)])

    starts = [d_share * c // CHUNK_UNITS for c in CHUNKS]
    chunks = [(d0, d1 - d0) for d0, d1 in zip(starts, [*starts[1:], d_share])]
    arrived = []
    turn = ids
    for c, (d0, dn) in enumerate(chunks):
        pieces = slice_chunk(after(ids, turn), flipped, owners, d0, dn)
        arrived.append(exchange(pieces))
        turn = pieces[0]
        if c == 0:
            window = cycle_window(after(ids, turn), live_pairs, flipped, A_WINDOW)
            windows = exchange([window] * (owners - 1))
            turn = window

    send, keep = cycle_product(window, windows, cycle_ints)
    recv = swap_pair(send)
    own, *sends = add_blocks(keep, recv, owners)
    blocks = [own, *exchange(sends)]
    cycle = small(functools.partial(place_kernel, owner_cols), sds(owner_rows, own.shape[1]), blocks)

    parts = fetch_integrals(after(ids, own), ladder_ints, chunks[-1][0])
    pair, denominator, live_out = setup(after(ids, parts[0]), live_pairs, occ_energy, vir_energy, pair_ints)
    far = chunks[2][0]
    (acc,) = ladder_product(after(ids, pair), [[flipped]], ladder_ints, far, lanes=True)
    own_send, own_keep, acc = ladder_product(ids, arrived[:2], ladder_ints, 0, own=flipped, acc=acc)
    own_recv = swap_pair(own_send)
    far_send, far_keep = ladder_product(ids, arrived[2:-1], ladder_ints, far, acc=acc)

    def closing(turn, hi, lo, acc):
        operands = [turn, *arrived[-1], hi, lo, acc]
        return small(functools.partial(closing_kernel, len(arrived[-1])), sds(*acc.shape), operands)

    far_send = closing(ids, *parts[:2], far_send)
    far_recv = swap_pair(far_send)
    far_keep = closing(after(ids, far_send), *parts[2:], far_keep)
    lines = sections // 2
    n = owners - 1
    sends = small(
        functools.partial(pair_pieces_kernel, n),
        [sds(owner_rows, (lines - 1) * LANES)] * n + [sds(owner_rows, LANES)] * n,
        [far_keep, far_recv],
    )
    far_terms = exchange(sends[:n])
    near_terms = exchange(sends[n:])
    order = list(reversed(range(lines)))

    def line(distances, terms):
        return small(
            functools.partial(line_kernel, n, distances),
            [sds(owner_rows, LANES)] * len(distances),
            [cycle, own_keep, own_recv, *terms],
        )

    def along(distances, pieces):
        return [
            lax.ppermute(piece, "sec", [(s, s ^ (2 * q)) for s in range(sections)])
            for q, piece in zip(distances, pieces)
        ]

    pieces = line(order[:-1], far_terms)
    recvs = along(order[:-1], pieces)
    (own_piece,) = line(order[-1:], near_terms)

    operands = [own_piece, *recvs, pair, denominator, live_out]
    return small(final_kernel, sds(*pair_ints.shape), operands)


def gathered(amplitudes, live_pairs, ladder_ints, cycle_ints, pair_ints, occ_energy, vir_energy):
    owners = lax.axis_size("occ")
    sections = lax.axis_size("sec")
    owner_index = lax.axis_index("occ")
    section = lax.axis_index("sec")
    owner_rows = I_OWNER * OCCUPIED
    window_rows = I_OWNER * owners
    owner_cols = OCCUPIED // owners
    col_share = A_WINDOW * B_WINDOW // sections
    d_share = amplitudes.shape[2]
    live_count = lax.dynamic_slice_in_dim(live_pairs, owner_index, 1)[0]
    local_rows = lax.broadcasted_iota(jnp.int32, (owner_rows, 1, 1), 0)
    live_rows = (local_rows < live_count).astype(jnp.float32)
    masked = amplitudes * live_rows
    flat_tiles = masked.reshape(owner_rows, owners, VIRTUAL // owners * d_share)
    regrouped = lax.all_to_all(flat_tiles, "occ", split_axis=1, concat_axis=0, tiled=True)
    pair_total = regrouped.shape[0]
    ladder_part = 0.5 * jnp.dot(
        regrouped.reshape(pair_total, -1),
        ladder_ints.reshape(-1, A_WINDOW * B_WINDOW),
        precision=highest,
        preferred_element_type=jnp.float32,
    )
    cycle_local = masked[:, :A_WINDOW, :].reshape(owner_rows, A_WINDOW * d_share)
    cycle_flat = lax.all_gather(cycle_local, "occ", axis=0, tiled=True)
    cycle_rows = cycle_flat.reshape(window_rows, OCCUPIED, A_WINDOW, d_share)
    cycle_part = jnp.einsum(
        "ikac,kcn->ian",
        cycle_rows,
        cycle_ints,
        precision=highest,
        preferred_element_type=jnp.float32,
    )
    cycle_part = (
        cycle_part.reshape(window_rows, A_WINDOW, owner_cols, B_WINDOW)
        .transpose(0, 2, 1, 3)
        .reshape(window_rows, owner_cols, A_WINDOW * B_WINDOW)
    )
    ladder_grid = ladder_part.reshape(window_rows, OCCUPIED, A_WINDOW * B_WINDOW)
    offset = owner_index * owner_cols
    current_part = lax.dynamic_slice_in_dim(ladder_grid, offset, owner_cols, 1)
    ladder_grid = lax.dynamic_update_slice_in_dim(ladder_grid, current_part + cycle_part, offset, 1)
    combined = ladder_grid.reshape(pair_total, A_WINDOW * B_WINDOW)
    first_sum = lax.psum_scatter(combined, "sec", scatter_dimension=1, tiled=True)
    summed = lax.psum_scatter(first_sum, "occ", scatter_dimension=0, tiled=True)
    residual = summed + pair_ints
    occ_rows = lax.dynamic_slice_in_dim(occ_energy, owner_index * I_OWNER, I_OWNER)
    pair_energy = (occ_rows[:, None] + occ_energy[None, :]).reshape(owner_rows, 1)
    vir_pairs = (vir_energy[:A_WINDOW, None] + vir_energy[None, :B_WINDOW]).reshape(
        A_WINDOW * B_WINDOW
    )
    vir_cols = lax.dynamic_slice_in_dim(vir_pairs, section * col_share, col_share)
    denominator = pair_energy - vir_cols[None, :]
    live_out = (lax.broadcasted_iota(jnp.int32, (owner_rows, 1), 0) < live_count).astype(
        jnp.float32
    )
    return residual / denominator * live_out


def power_of_two(n):
    return n & (n - 1) == 0


def streams(owners, sections):
    return (
        1 < owners
        and power_of_two(owners)
        and 2 < sections
        and power_of_two(sections)
        and VIRTUAL == owners * LANES
        and A_WINDOW * B_WINDOW == sections * LANES
        and B_WINDOW == LANES
        and OCCUPIED // owners <= CYCLE_PAD
        and A_WINDOW == D_STEP
        and LANES % (VIRTUAL // sections) == 0
        and sections // 2 == owners
        and VIRTUAL // sections % (D_STEP * CHUNK_UNITS) == 0
    )


def solution(mesh):
    in_specs = (
        P("occ", None, "sec"),
        P(),
        P("occ", "sec", None),
        P(None, "sec", "occ"),
        P("occ", "sec"),
        P(),
        P(),
    )
    out_specs = P("occ", "sec")
    if not streams(mesh.shape["occ"], mesh.shape["sec"]):
        return jax.shard_map(gathered, mesh=mesh, in_specs=in_specs, out_specs=out_specs, check_vma=False)
    return jax.shard_map(streamed_parts, mesh=mesh, in_specs=in_specs, out_specs=out_specs, check_vma=False)
```
